512 devices in a mesh: gx: 16 (over z, core), gy: 32 (over y, x).
Axes of the slice: x: 4, y: 8, z: 8, core: 2. Of those that a mesh axis runs over, the one named last changes fastest.
Arguments:
- source: float32 [128, 256, 512], P('gx', 'gy'), may hold values from -60 to 60
- conductivity: float32 [128, 256, 512], P('gx', 'gy'), may hold values from 0.5 to 5
- robin_flags: int32 [16, 32, 64], P('gx', 'gy'), may hold values from 0 to 63
- htc_class: int32 [16, 32, 64], P('gx', 'gy'), may hold values from 0 to 3
- htc_table: float32 [4], replicated, may hold values from 0.5 to 8
Outputs:
- adjoint: float32 [128, 256, 512], P('gx', 'gy')
- residual: float32 [128, 256, 512], P('gx', 'gy')
The draws below stay inside these ranges and needn't reach their ends.
Inputs may be any that keep to these rules, and one draw needn't show every extreme that they name: `robin_flags`: bit f (value 2^f) flags face f of the element, in the order x-min, x-max, y-min, y-max, z-min, z-max.
All inputs are finite; a program needn't handle non-finite values.
Results may differ from the reference program's by a relative error of at most 0.0003.
Values sent between devices are 32-bit elements; how exact they have to be, the bound alone decides.
A program may use at most 64 MiB of HBM per device.

```python
import math
import jax
import jax.numpy as jnp
import numpy as np
from jax import lax

CLASSES = 4
ITERS = 3
EZ = 64
NEX = 16
NEY = 32


def draw_source(key, part):
    shape_all = (8 * NEX, 8 * NEY, 8 * EZ)
    noise = jax.random.normal(jax.random.fold_in(key, 11), shape_all, jnp.float32)
    rough_part = 10.0 * noise
    return jnp.clip(rough_part, -60.0, 60.0)


def plant(values, stream_key, smallest, high):
    dims = values.shape
    index_at = [jax.random.randint(jax.random.fold_in(stream_key, axis), (), 0, dims[axis]) for axis in range(len(dims))]
    values = values.at[tuple(index_at)].set(smallest)
    longest = dims.index(max(dims))
    index_at[longest] = (index_at[longest] + 1) % dims[longest]
    return values.at[tuple(index_at)].set(high)


def level_of(stream_key, dims, split, least, top_value):
    def one(dim, shards_of):
        steps = jax.random.uniform(jax.random.fold_in(jax.random.fold_in(stream_key, 6), dim), (shards_of,), jnp.float32, least / len(split), top_value / len(split))
        return jnp.repeat(jnp.exp(steps), dims[dim] // shards_of).reshape((-1,) + (1,) * (len(dims) - dim - 1))

    factor_of = one(*split[0])
    for cut in split[1:]:
        factor_of = factor_of * one(*cut)
    return factor_of


def setup_inputs(seed: int = 0) -> dict:
    key_of = jax.random.split(jax.random.key(seed), 6)
    source = draw_source(jax.random.fold_in(key_of[5], 71), 0)
    conductivity = jnp.clip(jnp.exp(math.log(5.0) - 2.3025851 * jax.random.uniform(key_of[1], (8 * NEX, 8 * NEY, 8 * EZ), jnp.float32) ** level_of(key_of[1], (8 * NEX, 8 * NEY, 8 * EZ), ((0, 16), (1, 32)), -0.2, 0.2)), 0.5, 5.0)
    robin_flags = plant(jax.random.randint(key_of[2], (NEX, NEY, EZ), 0, 64), jax.random.fold_in(key_of[2], 1), 0, 63).astype(jnp.int32)
    htc_class = plant(jax.random.randint(key_of[3], (NEX, NEY, EZ), 0, CLASSES), jax.random.fold_in(key_of[3], 1), 0, CLASSES - 1).astype(jnp.int32)
    htc_table = jnp.clip(jnp.exp(jax.random.uniform(key_of[4], (CLASSES,), jnp.float32, math.log(0.5), math.log(8.0))), 0.5, 8.0)
    return dict(source=source, conductivity=conductivity, robin_flags=robin_flags, htc_class=htc_class, htc_table=htc_table)


gll_points = (-1.0, -0.8717401485096066, -0.5917001814331423, -0.2092992179024789, 0.2092992179024789, 0.5917001814331423, 0.8717401485096066, 1.0)
gll_weights = (0.03571428571428571, 0.21070422714350603, 0.3411226924835044, 0.4124587946587038, 0.4124587946587038, 0.3411226924835044, 0.21070422714350603, 0.03571428571428571)
mass_coef = 0.2
scan_speed = 2.0
highest = lax.Precision.HIGHEST


def lagrange_derivative():
    points = np.array(gll_points)
    barycentric = np.array([1.0 / np.prod([points[j] - points[m] for m in range(8) if m != j]) for j in range(8)])
    derivative = np.zeros((8, 8))
    for a in range(8):
        for b in range(8):
            if a != b:
                derivative[a, b] = barycentric[b] / barycentric[a] / (points[a] - points[b])
        derivative[a, a] = -np.sum(derivative[a])
    return jnp.asarray(derivative, jnp.float32)


def edge_weights(elements):
    return jnp.tile(jnp.asarray(np.array(gll_weights), jnp.float32), elements)


def copies_along(elements, first_element, total_elements):
    node_index = jnp.arange(8 * elements) % 8
    element_index = first_element + jnp.arange(8 * elements) // 8
    shared = ((node_index == 7) & (element_index < total_elements - 1)) | ((node_index == 0) & (element_index > 0))
    return jnp.where(shared, 2.0, 1.0).astype(jnp.float32)


def fold_inside(values, which_axis):
    moved_field = jnp.moveaxis(values, which_axis, 0)
    extent = moved_field.shape
    blocks = moved_field.reshape((extent[0] // 8, 8) + extent[1:])
    shared = blocks[:-1, 7] + blocks[1:, 0]
    blocks = blocks.at[:-1, 7].set(shared).at[1:, 0].set(shared)
    return jnp.moveaxis(blocks.reshape(extent), 0, which_axis)


def assemble(values):
    return fold_inside(fold_inside(fold_inside(values, 0), 1), 2)


def slab_operator(pieces, derivative, weight_y, weight_z):
    values, conduct_slab, robin_slab = pieces
    weight_x = edge_weights(1)
    weights = weight_x[:, None, None] * weight_y[None, :, None] * weight_z[None, None, :]
    size_y = values.shape[1]
    size_z = values.shape[2]
    grad_x = jnp.einsum("ij,jbc->ibc", derivative, values, precision=highest)
    grad_y = jnp.einsum("ij,anjc->anic", derivative, values.reshape(8, size_y // 8, 8, size_z), precision=highest).reshape(values.shape)
    grad_z = jnp.einsum("abkj,ij->abki", values.reshape(8, size_y, size_z // 8, 8), derivative, precision=highest).reshape(values.shape)
    flux_x = weights * (conduct_slab * grad_x - scan_speed * values)
    flux_y = weights * conduct_slab * grad_y
    flux_z = weights * conduct_slab * grad_z
    back_x = jnp.einsum("ij,ibc->jbc", derivative, flux_x, precision=highest)
    back_y = jnp.einsum("ij,anic->anjc", derivative, flux_y.reshape(8, size_y // 8, 8, size_z), precision=highest).reshape(values.shape)
    back_z = jnp.einsum("abki,ij->abkj", flux_z.reshape(8, size_y, size_z // 8, 8), derivative, precision=highest).reshape(values.shape)
    return mass_coef * weights * values + robin_slab * values + back_x + back_y + back_z


def reference_robin(robin_flags, htc_class, htc_table):
    class_hits = (htc_class[..., None] == jnp.arange(CLASSES)).astype(jnp.float32)
    coefficient = jnp.sum(class_hits * htc_table, axis=-1)
    index_x = jnp.arange(NEX)[:, None, None]
    index_y = jnp.arange(NEY)[None, :, None]
    index_z = jnp.arange(EZ)[None, None, :]
    boundary = [index_x == 0, index_x == NEX - 1, index_y == 0, index_y == NEY - 1, index_z == 0, index_z == EZ - 1]
    weight_x = edge_weights(NEX)
    weight_y = edge_weights(NEY)
    weight_z = edge_weights(EZ)
    node_x = (jnp.arange(8 * NEX) % 8)[:, None, None]
    node_y = (jnp.arange(8 * NEY) % 8)[None, :, None]
    node_z = (jnp.arange(8 * EZ) % 8)[None, None, :]
    cross_x = weight_y[None, :, None] * weight_z[None, None, :]
    cross_y = weight_x[:, None, None] * weight_z[None, None, :]
    cross_z = weight_x[:, None, None] * weight_y[None, :, None]
    patterns = [(node_x == 0) * cross_x, (node_x == 7) * cross_x, (node_y == 0) * cross_y, (node_y == 7) * cross_y, (node_z == 0) * cross_z, (node_z == 7) * cross_z]
    robin_sum = jnp.zeros((8 * NEX, 8 * NEY, 8 * EZ), jnp.float32)
    for face_bit in range(6):
        flag_bit = ((robin_flags // (1 << face_bit)) % 2).astype(jnp.float32)
        coef_face = coefficient * flag_bit * boundary[face_bit].astype(jnp.float32)
        spread = jnp.repeat(jnp.repeat(jnp.repeat(coef_face, 8, axis=0), 8, axis=1), 8, axis=2)
        robin_sum = robin_sum + spread * patterns[face_bit].astype(jnp.float32)
    return robin_sum


def reference(source, conductivity, robin_flags, htc_class, htc_table):
    derivative = lagrange_derivative()
    weight_x = edge_weights(NEX)
    weight_y = edge_weights(NEY)
    weight_z = edge_weights(EZ)
    copies_x = copies_along(NEX, 0, NEX)
    copies_y = copies_along(NEY, 0, NEY)
    copies_z = copies_along(EZ, 0, EZ)
    inv_copies = 1.0 / (copies_x[:, None, None] * copies_y[None, :, None] * copies_z[None, None, :])
    robin_diag = reference_robin(robin_flags, htc_class, htc_table)
    slab_shape = (NEX, 8, 8 * NEY, 8 * EZ)

    def operate(values):
        stacked = (values.reshape(slab_shape), conductivity.reshape(slab_shape), robin_diag.reshape(slab_shape))
        local_terms = lax.map(lambda pieces: slab_operator(pieces, derivative, weight_y, weight_z), stacked)
        return assemble(local_terms.reshape(values.shape))

    def inner(left, right):
        return jnp.sum(left * right * inv_copies)

    weights = weight_x[:, None, None] * weight_y[None, :, None] * weight_z[None, None, :]
    assembled = assemble(weights * source)
    adjoint = jnp.zeros_like(assembled)
    residual = assembled
    direction = assembled
    rho_now = inner(assembled, assembled)
    for iteration in range(ITERS):
        applied = operate(direction)
        alpha_step = rho_now / inner(assembled, applied)
        half_resid = residual - alpha_step * applied
        applied_half = operate(half_resid)
        omega_step = inner(applied_half, half_resid) / inner(applied_half, applied_half)
        adjoint = adjoint + alpha_step * direction + omega_step * half_resid
        residual = half_resid - omega_step * applied_half
        rho_next = inner(assembled, residual)
        beta_step = (rho_next / rho_now) * (alpha_step / omega_step)
        direction = residual + beta_step * (direction - omega_step * applied)
        rho_now = rho_next
    return adjoint, residual
```

```python
import functools

import jax
import jax.numpy as jnp
import numpy as np
from jax import lax
from jax.experimental import pallas as pl
from jax.experimental.pallas import tpu as pltpu
from jax.sharding import PartitionSpec as P

MESH = pl.DeviceIdType.MESH
HIGHEST = lax.Precision.HIGHEST
f32 = jnp.float32

gll_points = (
    -1.0,
    -0.8717401485096066,
    -0.5917001814331423,
    -0.2092992179024789,
    0.2092992179024789,
    0.5917001814331423,
    0.8717401485096066,
    1.0,
)
gll_weights = (
    0.03571428571428571,
    0.21070422714350603,
    0.3411226924835044,
    0.4124587946587038,
    0.4124587946587038,
    0.3411226924835044,
    0.21070422714350603,
    0.03571428571428571,
)
mass_coef = 0.2
scan_speed = 2.0
ROUNDS = 7
SUMS = 3


def derivative_matrix():
    points = np.array(gll_points)
    bary = np.array(
        [1.0 / np.prod([points[j] - points[m] for m in range(8) if m != j]) for j in range(8)]
    )
    d = np.zeros((8, 8))
    for a in range(8):
        for b in range(8):
            if a != b:
                d[a, b] = bary[b] / bary[a] / (points[a] - points[b])
        d[a, a] = -np.sum(d[a])
    return d


D = derivative_matrix()


def along_planes(planes, mat):
    even = [planes[b] + planes[7 - b] for b in range(4)]
    odd = [planes[b] - planes[7 - b] for b in range(4)]
    out = [None] * 8
    for a in range(4):
        p = sum(float(0.5 * (mat[a, b] + mat[a, 7 - b])) * even[b] for b in range(4))
        q = sum(float(0.5 * (mat[a, b] - mat[a, 7 - b])) * odd[b] for b in range(4))
        out[a] = p + q
        out[7 - a] = q - p
    return out


def kernel(
    nx, ny, nz,
    src_hbm, cond_hbm, flags_hbm, class_hbm, table_ref, mats_hbm, kmat_hbm, planes_hbm,
    adj_ref, res_ref,
    src, wk, flags, classes, mats, kmat, planes, mass, im,
    loc, vec, xr, yr, cr, ysend, csend,
    parts, msg1, msg2, buf1, buf2,
    in_sem, send_x, send_y, send_c, recv_x, recv_y, recv_c,
    send_1, send_2, recv_1, recv_2,
):
    gx = lax.axis_index("gx")
    gy = lax.axis_index("gy")

    def at_x(k):
        return lax.rem(gx + (k % nx), nx)

    def at_y(k):
        return lax.rem(gy + (k % ny), ny)

    loads = [
        pltpu.make_async_copy(a, b, in_sem.at[i])
        for i, (a, b) in enumerate(
            [
                (planes_hbm, planes),
                (src_hbm, src),
                (cond_hbm, wk),
                (flags_hbm, flags),
                (class_hbm, classes),
                (mats_hbm, mats),
                (kmat_hbm, kmat),
            ]
        )
    ]
    for c in loads:
        c.start()

    barrier = pltpu.get_barrier_semaphore()
    order_x = sorted(range(1, nx), key=lambda k: abs(k - nx // 2))
    order_y = sorted(range(1, ny), key=lambda k: abs(k - ny // 2))
    peers = [(at_x(dx), at_y(dy)) for dx in (-1, 1) for dy in (-1, 1)]
    peers += [(gx, at_y(k)) for k in order_y] + [(at_x(k), gy) for k in order_x]
    for peer in peers:
        pl.semaphore_signal(barrier, inc=1, device_id=peer, device_id_type=MESH)

    lane = lax.broadcasted_iota(jnp.int32, (8, nz), 1)
    node_z = lax.rem(lane, 8)
    row = lax.broadcasted_iota(jnp.int32, (8, nz), 0)
    join_up = (node_z == 7) & (lane < nz - 1)
    join_dn = (node_z == 0) & (lane > 0)
    zero = jnp.zeros((8, nz), f32)
    x_lo, x_hi = gx > 0, gx < nx - 1
    y_lo, y_hi = gy > 0, gy < ny - 1

    def zfold(plane):
        up = pltpu.roll(plane, nz - 1, 1)
        dn = pltpu.roll(plane, 1, 1)
        return plane + jnp.where(join_up, up, jnp.where(join_dn, dn, zero))

    for c in loads[:2]:
        c.wait()
    w_yz = planes[0]
    inv_z = planes[1]

    def put_local(k, x, plane):
        loc[k, x] = plane
        ysend[k, 0, pl.ds(x, 1), :] = plane[0:1]
        ysend[k, 1, pl.ds(x, 1), :] = plane[7:8]
        if x in (0, 7):
            csend[k, 0 if x == 0 else 2] = plane[0:1]
            csend[k, 1 if x == 0 else 3] = plane[7:8]

    def halo_start(k):
        def send(s, d, ss, rs, peer):
            pltpu.make_async_remote_copy(
                src_ref=s, dst_ref=d, send_sem=ss, recv_sem=rs,
                device_id=peer, device_id_type=MESH,
            ).start()

        for i, (dx, dy) in enumerate(((-1, -1), (-1, 1), (1, -1), (1, 1))):
            send(csend.at[k, i], cr.at[k, 3 - i], send_c, recv_c.at[k], (at_x(dx), at_y(dy)))
        for i, dy in enumerate((-1, 1)):
            send(ysend.at[k, i], yr.at[k, 1 - i], send_y, recv_y.at[k], (gx, at_y(dy)))
        for i, dx in enumerate((-1, 1)):
            send(loc.at[k, 7 * i], xr.at[k, 1 - i], send_x, recv_x.at[k], (at_x(dx), gy))

    def halo_wait(k):
        pltpu.make_async_copy(xr.at[k], xr.at[k], recv_x.at[k]).wait()
        pltpu.make_async_copy(yr.at[k], yr.at[k], recv_y.at[k]).wait()
        pltpu.make_async_copy(cr.at[k], cr.at[k], recv_c.at[k]).wait()

    def assembled_plane(k, x):
        plane = loc[k, x]
        lo = jnp.broadcast_to(yr[k, 0, pl.ds(x, 1), :], (8, nz))
        hi = jnp.broadcast_to(yr[k, 1, pl.ds(x, 1), :], (8, nz))
        if x in (0, 7):
            i = 0 if x == 0 else 1
            has = x_lo if x == 0 else x_hi
            lo = lo + jnp.where(has, jnp.broadcast_to(cr[k, 2 * i], (8, nz)), zero)
            hi = hi + jnp.where(has, jnp.broadcast_to(cr[k, 2 * i + 1], (8, nz)), zero)
            plane = plane + jnp.where(has, xr[k, i], zero)
        add = jnp.where((row == 0) & y_lo, lo, jnp.where((row == 7) & y_hi, hi, zero))
        return plane + add

    def halo_finish(k, dst):
        halo_wait(k)
        for x in range(8):
            vec[dst, x] = assembled_plane(k, x)

    for x in range(8):
        put_local(0, x, zfold(float(gll_weights[x]) * w_yz * src[x]))

    for c in loads[2:]:
        c.wait()
    bits = flags[...]
    kinds = classes[...]
    coef = jnp.zeros(kinds.shape, f32)
    for i in range(4):
        coef = coef + jnp.where(kinds == i, table_ref[i], 0.0)

    pl.semaphore_wait(barrier, len(peers))
    halo_start(0)

    edge = [gx == 0, gx == nx - 1, gy == 0, gy == ny - 1]
    faces = []
    for i in range(6):
        bit = lax.bitwise_and(lax.shift_right_logical(bits, i), 1).astype(f32)
        face = coef * bit
        if i < 4:
            face = jnp.where(edge[i], face, 0.0)
        faces.append(face)
    faces = jnp.concatenate(faces + [jnp.zeros((2, kinds.shape[1]), f32)], axis=0)
    elem = lax.broadcasted_iota(jnp.int32, (kinds.shape[1], nz), 0)
    spread = (lax.broadcasted_iota(jnp.int32, (kinds.shape[1], nz), 1) // 8 == elem).astype(f32)
    wide = jnp.dot(faces, spread, precision=HIGHEST, preferred_element_type=f32)

    def line(i):
        return jnp.broadcast_to(wide[i : i + 1], (8, nz))

    w_y = planes[2]
    w_z = planes[3]
    side_y = jnp.where(row == 0, line(2), jnp.where(row == 7, line(3), zero)) * w_z
    side_z = jnp.where(lane == 0, line(4), jnp.where(lane == nz - 1, line(5), zero)) * w_y
    inv_y = jnp.where(((row == 0) & y_lo) | ((row == 7) & y_hi), 0.5, 1.0).astype(f32)
    inv_yz = inv_y * inv_z
    for x in range(8):
        wx = float(gll_weights[x])
        robin = wx * (side_y + side_z)
        inv = inv_yz
        if x == 0:
            robin = robin + line(0) * w_yz
            inv = jnp.where(x_lo, 0.5 * inv_yz, inv_yz)
        if x == 7:
            robin = robin + line(1) * w_yz
            inv = jnp.where(x_hi, 0.5 * inv_yz, inv_yz)
        mass[x] = (mass_coef * wx) * w_yz + robin
        im[x] = inv
        wk[x] = (wx * w_yz) * wk[x]

    chunks = [slice(128 * t, 128 * t + 128) for t in range(nz // 128)]

    def apply_local(s, k):
        v = [vec[s, x] for x in range(8)]
        grad_x = along_planes(v, D)
        flux_x = [
            wk[x] * grad_x[x] - (scan_speed * float(gll_weights[x])) * (w_yz * v[x])
            for x in range(8)
        ]
        back_x = along_planes(flux_x, D.T)
        acc = [mass[x] * v[x] + back_x[x] for x in range(8)]
        whole = vec[s].reshape(64, nz)
        wk2 = wk[...].reshape(64, nz)
        grad_y = jnp.dot(kmat[0], whole, precision=HIGHEST, preferred_element_type=f32)
        back = jnp.dot(kmat[1], wk2 * grad_y, precision=HIGHEST, preferred_element_type=f32)
        tall = jnp.concatenate([whole[:, c] for c in chunks], axis=0)
        wk_t = jnp.concatenate([wk2[:, c] for c in chunks], axis=0)
        grad_z = jnp.dot(tall, mats[0], precision=HIGHEST, preferred_element_type=f32)
        back_z = jnp.dot(wk_t * grad_z, mats[1], precision=HIGHEST, preferred_element_type=f32)
        back_z = jnp.concatenate(
            [back_z[64 * t : 64 * t + 64] for t in range(len(chunks))], axis=1
        )
        back = (back + back_z).reshape(8, 8, nz)
        for x in range(8):
            put_local(k, x, zfold(acc[x] + back[x]))

    parts[...] = jnp.zeros(parts.shape, f32)
    ones = jnp.ones((8, 128), f32)

    def put_dot(j, d, left, right):
        total = sum(left[x] * right[x] for x in range(8))
        parts[j, 8 * d : 8 * d + 8, :] = sum(total[:, c] for c in chunks)

    def planes_of(s):
        return [vec[s, x] for x in range(8)]

    def weighted(v):
        return [im[x] * v[x] for x in range(8)]

    def sum_start(j):
        rows = lax.dot_general(
            ones, parts[j], (((1,), (1,)), ((), ())),
            precision=HIGHEST, preferred_element_type=f32,
        )
        msg1[j] = rows[0:1]
        buf1[j, pl.ds(gx, 1)] = rows[0:1].reshape(1, 1, 128)
        for k in order_x:
            pltpu.make_async_remote_copy(
                src_ref=msg1.at[j], dst_ref=buf1.at[j, gx], send_sem=send_1,
                recv_sem=recv_1.at[j], device_id=(at_x(k), gy), device_id_type=MESH,
            ).start()

    def sum_middle(j):
        pltpu.make_async_copy(
            buf1.at[j, pl.ds(0, nx - 1)], buf1.at[j, pl.ds(0, nx - 1)], recv_1.at[j]
        ).wait()
        total = jnp.sum(buf1[j], axis=0)
        msg2[j] = total
        buf2[j, pl.ds(gy, 1)] = total.reshape(1, 1, 128)
        for k in order_y:
            pltpu.make_async_remote_copy(
                src_ref=msg2.at[j], dst_ref=buf2.at[j, gy], send_sem=send_2,
                recv_sem=recv_2.at[j], device_id=(gx, at_y(k)), device_id_type=MESH,
            ).start()

    pick = (
        lax.broadcasted_iota(jnp.int32, (16, 128), 1) // 8
        == lax.broadcasted_iota(jnp.int32, (16, 128), 0)
    )

    def sum_finish(j):
        pltpu.make_async_copy(
            buf2.at[j, pl.ds(0, ny - 1)], buf2.at[j, pl.ds(0, ny - 1)], recv_2.at[j]
        ).wait()
        total = jnp.broadcast_to(jnp.sum(buf2[j], axis=0), (16, 128))
        spread_rows = jnp.where(pick, total, 0.0)
        return jnp.dot(
            spread_rows, jnp.ones((128, 128), f32), precision=HIGHEST,
            preferred_element_type=f32,
        )

    def wide_of(scalar):
        return jnp.broadcast_to(jnp.concatenate([scalar] * len(chunks), axis=1), (8, nz))

    B, V1, V2, V3, V4, R, RA, RA2, RA3, PP, PA, PA2, PA3, PA4, X = range(15)

    halo_finish(0, B)
    apply_local(B, 1)
    halo_start(1)
    b = planes_of(B)
    bw = weighted(b)
    put_dot(0, 0, bw, b)
    halo_finish(1, V1)
    apply_local(V1, 2)
    halo_start(2)
    v1 = planes_of(V1)
    put_dot(0, 1, weighted(planes_of(B)), v1)
    put_dot(0, 2, weighted(v1), v1)
    halo_finish(2, V2)
    v2 = planes_of(V2)
    v2w = weighted(v2)
    put_dot(0, 3, v2w, planes_of(B))
    put_dot(0, 4, v2w, planes_of(V1))
    put_dot(0, 5, v2w, v2)
    sum_start(0)
    apply_local(V2, 3)
    halo_start(3)
    sum_middle(0)
    halo_finish(3, V3)
    apply_local(V3, 4)
    halo_start(4)
    halo_finish(4, V4)

    s = sum_finish(0)
    bb, bv1, v1v1, bv2, v1v2, v2v2 = [s[i : i + 1] for i in range(6)]
    rho = bb
    alpha = rho / bv1
    cross = bv1 - alpha * (v1v1 + bv2) + alpha * alpha * v1v2
    square = v1v1 - 2.0 * alpha * v1v2 + alpha * alpha * v2v2
    omega = cross / square
    rho_next = -omega * (bv1 - alpha * bv2)
    beta = rho_next / rho * (alpha / omega)
    rho = rho_next
    al, om, be = wide_of(alpha), wide_of(omega), wide_of(beta)
    for x in range(8):
        b, v1, v2, v3, v4 = [vec[i, x] for i in (B, V1, V2, V3, V4)]
        s0 = b - al * v1
        s1 = v1 - al * v2
        s2 = v2 - al * v3
        s3 = v3 - al * v4
        vec[X, x] = al * b + om * s0
        r0 = s0 - om * s1
        r1 = s1 - om * s2
        r2 = s2 - om * s3
        vec[R, x] = r0
        vec[RA, x] = r1
        vec[RA2, x] = r2
        vec[PP, x] = r0 + be * (b - om * v1)
        vec[PA, x] = r1 + be * (v1 - om * v2)
        vec[PA2, x] = r2 + be * (v2 - om * v3)

    def put_dots(j):
        ra = planes_of(RA)
        raw = weighted(ra)
        put_dot(j, 0, raw, planes_of(R))
        put_dot(j, 1, raw, planes_of(PA))
        put_dot(j, 2, raw, ra)
        pa2 = planes_of(PA2)
        pa2w = weighted(pa2)
        put_dot(j, 3, pa2w, planes_of(R))
        put_dot(j, 4, pa2w, planes_of(PA))
        put_dot(j, 5, pa2w, ra)
        put_dot(j, 6, pa2w, pa2)
        bw = weighted(planes_of(B))
        put_dot(j, 7, bw, planes_of(PA))
        if j == 1:
            put_dot(j, 8, bw, ra)
            put_dot(j, 9, bw, pa2)

    def steps(j, rho):
        s = sum_finish(j)
        (ra_r, ra_pa, ra_ra, p2_r, p2_pa, p2_ra, p2_p2, b_pa, b_ra, b_p2) = [
            s[i : i + 1] for i in range(10)
        ]
        alpha = rho / b_pa
        cross = ra_r - alpha * (ra_pa + p2_r) + alpha * alpha * p2_pa
        square = ra_ra - 2.0 * alpha * p2_ra + alpha * alpha * p2_p2
        omega = cross / square
        rho_next = -omega * (b_ra - alpha * b_p2)
        beta = rho_next / rho * (alpha / omega)
        return alpha, omega, beta, rho_next

    put_dots(1)
    sum_start(1)
    apply_local(PA2, 5)
    halo_start(5)
    sum_middle(1)
    halo_finish(5, PA3)
    apply_local(PA3, 6)
    halo_start(6)
    for x in range(8):
        vec[RA3, x] = vec[PA3, x] - be * (vec[V3, x] - om * vec[V4, x])
    halo_finish(6, PA4)

    alpha, omega, beta, rho = steps(1, rho)
    al, om, be = wide_of(alpha), wide_of(omega), wide_of(beta)
    for x in range(8):
        r0, r1, r2, r3 = [vec[i, x] for i in (R, RA, RA2, RA3)]
        p0, p1, p2, p3, p4 = [vec[i, x] for i in (PP, PA, PA2, PA3, PA4)]
        s0 = r0 - al * p1
        s1 = r1 - al * p2
        s2 = r2 - al * p3
        s3 = r3 - al * p4
        vec[X, x] = vec[X, x] + al * p0 + om * s0
        r0 = s0 - om * s1
        r1 = s1 - om * s2
        r2 = s2 - om * s3
        vec[R, x] = r0
        vec[RA, x] = r1
        vec[PP, x] = r0 + be * (p0 - om * p1)
        vec[PA, x] = r1 + be * (p1 - om * p2)
        vec[PA2, x] = r2 + be * (p2 - om * p3)

    put_dots(2)
    sum_start(2)
    sum_middle(2)
    alpha, omega, _, _ = steps(2, rho)
    al, om = wide_of(alpha), wide_of(omega)
    for x in range(8):
        s0 = vec[R, x] - al * vec[PA, x]
        s1 = vec[RA, x] - al * vec[PA2, x]
        adj_ref[x] = vec[X, x] + al * vec[PP, x] + om * s0
        res_ref[x] = s0 - om * s1

    pltpu.make_async_copy(xr, xr, send_x).wait()
    pltpu.make_async_copy(yr, yr, send_y).wait()
    pltpu.make_async_copy(cr, cr, send_c).wait()
    sent_1 = buf1.at[:, pl.ds(0, nx - 1)]
    pltpu.make_async_copy(sent_1, sent_1, send_1).wait()
    sent_2 = buf2.at[:, pl.ds(0, ny - 1)]
    pltpu.make_async_copy(sent_2, sent_2, send_2).wait()


def constants(nz):
    w = np.array(gll_weights)
    wz = np.tile(w, nz // 8)
    node = np.arange(nz) % 8
    elem = np.arange(nz) // 8
    shared = ((node == 7) & (elem < nz // 8 - 1)) | ((node == 0) & (elem > 0))
    inv_z = np.where(shared, 0.5, 1.0)
    planes = np.stack(
        [
            w[:, None] * wz[None, :],
            np.broadcast_to(inv_z, (8, nz)),
            np.broadcast_to(w[:, None], (8, nz)),
            np.broadcast_to(wz, (8, nz)),
        ]
    ).astype(np.float32)
    block = np.kron(np.eye(16), D)
    mats = np.stack([block.T, block]).astype(np.float32)
    along_y = np.kron(np.eye(8), D)
    kmat = np.stack([along_y, along_y.T]).astype(np.float32)
    return mats, kmat, planes


def solution(mesh):
    nx, ny = mesh.shape["gx"], mesh.shape["gy"]

    def per_device(source, conductivity, robin_flags, htc_class, htc_table):
        nz = source.shape[2]
        ez = robin_flags.shape[2]
        mats, kmat, planes = constants(nz)
        any_spec = pl.BlockSpec(memory_space=pl.ANY)
        vm = pltpu.VMEM
        dma = pltpu.SemaphoreType.DMA
        field = (8, 8, nz)
        return pl.pallas_call(
            functools.partial(kernel, nx, ny, nz),
            out_shape=(jax.ShapeDtypeStruct(field, f32), jax.ShapeDtypeStruct(field, f32)),
            in_specs=[any_spec] * 4
            + [pl.BlockSpec(memory_space=pltpu.SMEM)]
            + [any_spec] * 3,
            out_specs=(pl.BlockSpec(memory_space=pltpu.VMEM),) * 2,
            scratch_shapes=[
                vm(field, f32),
                vm(field, f32),
                vm((1, ez), jnp.int32),
                vm((1, ez), jnp.int32),
                vm((2, 128, 128), f32),
                vm((2, 64, 64), f32),
                vm((4, 8, nz), f32),
                vm(field, f32),
                vm(field, f32),
                vm((ROUNDS,) + field, f32),
                vm((15,) + field, f32),
                vm((ROUNDS, 2, 8, nz), f32),
                vm((ROUNDS, 2, 8, nz), f32),
                vm((ROUNDS, 4, 1, nz), f32),
                vm((ROUNDS, 2, 8, nz), f32),
                vm((ROUNDS, 4, 1, nz), f32),
                vm((SUMS, 128, 128), f32),
                vm((SUMS, 1, 128), f32),
                vm((SUMS, 1, 128), f32),
                vm((SUMS, nx, 1, 128), f32),
                vm((SUMS, ny, 1, 128), f32),
                dma((7,)),
                dma,
                dma,
                dma,
                dma((ROUNDS,)),
                dma((ROUNDS,)),
                dma((ROUNDS,)),
                dma,
                dma,
                dma((SUMS,)),
                dma((SUMS,)),
            ],
            compiler_params=pltpu.CompilerParams(collective_id=0, has_side_effects=True),
        )(
            source,
            conductivity,
            robin_flags.reshape(1, ez),
            htc_class.reshape(1, ez),
            htc_table,
            mats,
            kmat,
            planes,
        )

    return jax.shard_map(
        per_device,
        mesh=mesh,
        in_specs=(
            P("gx", "gy", None),
            P("gx", "gy", None),
            P("gx", "gy", None),
            P("gx", "gy", None),
            P(),
        ),
        out_specs=(P("gx", "gy", None), P("gx", "gy", None)),
        check_vma=False,
    )
```

```python
import functools

import jax
import jax.numpy as jnp
import numpy as np
from jax import lax
from jax.experimental import pallas as pl
from jax.experimental.pallas import tpu as pltpu
from jax.sharding import PartitionSpec as P

MESH = pl.DeviceIdType.MESH
HIGHEST = lax.Precision.HIGHEST
f32 = jnp.float32

gll_points = (
    -1.0,
    -0.8717401485096066,
    -0.5917001814331423,
    -0.2092992179024789,
    0.2092992179024789,
    0.5917001814331423,
    0.8717401485096066,
    1.0,
)
gll_weights = (
    0.03571428571428571,
    0.21070422714350603,
    0.3411226924835044,
    0.4124587946587038,
    0.4124587946587038,
    0.3411226924835044,
    0.21070422714350603,
    0.03571428571428571,
)
mass_coef = 0.2
scan_speed = 2.0
ROUNDS = 7
SUMS = 3


def derivative_matrix():
    points = np.array(gll_points)
    bary = np.array(
        [1.0 / np.prod([points[j] - points[m] for m in range(8) if m != j]) for j in range(8)]
    )
    d = np.zeros((8, 8))
    for a in range(8):
        for b in range(8):
            if a != b:
                d[a, b] = bary[b] / bary[a] / (points[a] - points[b])
        d[a, a] = -np.sum(d[a])
    return d


D = derivative_matrix()


def along_planes(planes, mat):
    even = [planes[b] + planes[7 - b] for b in range(4)]
    odd = [planes[b] - planes[7 - b] for b in range(4)]
    out = [None] * 8
    for a in range(4):
        p = sum(float(0.5 * (mat[a, b] + mat[a, 7 - b])) * even[b] for b in range(4))
        q = sum(float(0.5 * (mat[a, b] - mat[a, 7 - b])) * odd[b] for b in range(4))
        out[a] = p + q
        out[7 - a] = q - p
    return out


def kernel(
    nx, ny, nz,
    src_hbm, cond_hbm, flags_hbm, class_hbm, table_hbm, mats_hbm, planes_hbm,
    adj_ref, res_ref,
    src, cond, wk, wkt, flags, classes, table, mats, planes, mass, im,
    loc, vec, tmp, xr, yr, cr, ysend,
    parts, msg1, msg2, buf1, buf2,
    in_sem, send_x, send_y, send_c, recv_x, recv_y, recv_c,
    send_1, send_2, recv_1, recv_2,
):
    gx = lax.axis_index("gx")
    gy = lax.axis_index("gy")

    def at_x(k):
        return (gx + (k % nx)) & (nx - 1)

    def at_y(k):
        return (gy + (k % ny)) & (ny - 1)

    loads = [
        pltpu.make_async_copy(a, b, in_sem.at[i])
        for i, (a, b) in enumerate(
            [
                (src_hbm, src),
                (planes_hbm, planes),
                (cond_hbm, cond),
                (mats_hbm, mats),
                (flags_hbm, flags),
                (class_hbm, classes),
                (table_hbm, table),
            ]
        )
    ]
    for c in loads[:2]:
        c.start()

    barrier = pltpu.get_barrier_semaphore()
    order_x = sorted(range(1, nx), key=lambda k: abs(k - nx // 2))
    order_y = sorted(range(1, ny), key=lambda k: abs(k - ny // 2))
    peers = [(at_x(dx), at_y(dy)) for dx in (-1, 1) for dy in (-1, 1)]
    peers += [(gx, at_y(k)) for k in order_y] + [(at_x(k), gy) for k in order_x]
    for peer in peers:
        pl.semaphore_signal(barrier, inc=1, device_id=peer, device_id_type=MESH)
    for c in loads[2:]:
        c.start()

    lane = lax.broadcasted_iota(jnp.int32, (8, nz), 1)
    node_z = lax.rem(lane, 8)
    row = lax.broadcasted_iota(jnp.int32, (8, nz), 0)
    join_up = (node_z == 7) & (lane < nz - 1)
    join_dn = (node_z == 0) & (lane > 0)
    zero = jnp.zeros((8, nz), f32)
    x_lo, x_hi = gx > 0, gx < nx - 1
    y_lo, y_hi = gy > 0, gy < ny - 1
    row_t = lax.broadcasted_iota(jnp.int32, (8, 128), 0)
    corner = ((row_t == 0) & x_lo) | ((row_t == 7) & x_hi)
    tile0 = jnp.zeros((8, 128), f32)
    chunks = [slice(128 * t, 128 * t + 128) for t in range(nz // 128)]

    def zfold(plane):
        up = pltpu.roll(plane, nz - 1, 1)
        dn = pltpu.roll(plane, 1, 1)
        return plane + jnp.where(join_up, up, jnp.where(join_dn, dn, zero))

    nt = len(chunks)

    def at(x):
        return slice(8 * x, 8 * x + 8)

    def get(ref, x):
        return jnp.concatenate([ref[t, at(x), :] for t in range(nt)], axis=1)

    def put(ref, x, plane):
        for t, c in enumerate(chunks):
            ref[t, at(x), :] = plane[:, c]

    def across(y):
        return pl.ds(y, 8, stride=8)

    for c in loads[:2]:
        c.wait()
    w_yz = planes[0]
    inv_z = planes[1]

    def halo_start(k):
        def send(s, d, ss, rs, peer):
            pltpu.make_async_remote_copy(
                src_ref=s, dst_ref=d, send_sem=ss, recv_sem=rs,
                device_id=peer, device_id_type=MESH,
            ).start()

        for dx, dy in ((-1, -1), (-1, 1), (1, -1), (1, 1)):
            mine = 56 * (dx > 0) + 7 * (dy > 0)
            send(
                loc.at[k, :, pl.ds(mine, 1), :],
                cr.at[k, int(dy < 0), :, pl.ds(7 * (dx < 0), 1), :],
                send_c, recv_c.at[k], (at_x(dx), at_y(dy)),
            )
        for i, dy in enumerate((-1, 1)):
            for t in range(nt):
                ysend[k, i, t] = loc.at[k, t][across(7 * i), :]
            send(ysend.at[k, i], yr.at[k, 1 - i], send_y, recv_y.at[k], (gx, at_y(dy)))
        for i, dx in enumerate((-1, 1)):
            send(
                loc.at[k, :, pl.ds(56 * i, 8), :], xr.at[k, 1 - i],
                send_x, recv_x.at[k], (at_x(dx), gy),
            )

    def halo_finish(k, dst):
        for t in range(nt):
            vec[dst, t, 8:56, :] = loc[k, t, 8:56, :]
        pltpu.make_async_copy(xr.at[k], xr.at[k], recv_x.at[k]).wait()
        for t in range(nt):
            vec[dst, t, at(0), :] = loc[k, t, at(0), :] + jnp.where(x_lo, xr[k, 0, t], tile0)
            vec[dst, t, at(7), :] = loc[k, t, at(7), :] + jnp.where(x_hi, xr[k, 1, t], tile0)
        pltpu.make_async_copy(yr.at[k], yr.at[k], recv_y.at[k]).wait()
        lines = cr.at[k, 0, :, pl.ds(0, 4), :]
        pltpu.make_async_copy(lines, lines, recv_c.at[k]).wait()
        for i, has in enumerate((y_lo, y_hi)):
            for t in range(nt):
                add = yr[k, i, t] + jnp.where(corner, cr[k, i, t], tile0)
                add = jnp.where(has, add, tile0)
                vec.at[dst, t][across(7 * i), :] = vec.at[dst, t][across(7 * i), :] + add

    for x in range(8):
        put(loc.at[0], x, zfold(float(gll_weights[x]) * w_yz * src[x]))

    pl.semaphore_wait(barrier, len(peers))
    halo_start(0)

    for c in loads[2:]:
        c.wait()
    bits = flags[...]
    kinds = classes[...]
    coef = jnp.zeros(kinds.shape, f32)
    for i in range(4):
        coef = coef + jnp.where(kinds == i, table[0, i], 0.0)
    edge = [gx == 0, gx == nx - 1, gy == 0, gy == ny - 1]
    faces = []
    for i in range(6):
        bit = lax.bitwise_and(lax.shift_right_logical(bits, i), 1).astype(f32)
        face = coef * bit
        if i < 4:
            face = jnp.where(edge[i], face, 0.0)
        faces.append(face)
    faces = jnp.concatenate(faces + [jnp.zeros((2, kinds.shape[1]), f32)], axis=0)
    elem = lax.broadcasted_iota(jnp.int32, (kinds.shape[1], nz), 0)
    spread = (lax.broadcasted_iota(jnp.int32, (kinds.shape[1], nz), 1) // 8 == elem).astype(f32)
    wide = jnp.dot(faces, spread, precision=HIGHEST, preferred_element_type=f32)

    def line(i):
        return jnp.broadcast_to(wide[i : i + 1], (8, nz))

    w_y = planes[2]
    w_z = planes[3]
    side_y = jnp.where(row == 0, line(2), jnp.where(row == 7, line(3), zero)) * w_z
    side_z = jnp.where(lane == 0, line(4), jnp.where(lane == nz - 1, line(5), zero)) * w_y
    inv_y = jnp.where(((row == 0) & y_lo) | ((row == 7) & y_hi), 0.5, 1.0).astype(f32)
    inv_yz = inv_y * inv_z
    for x in range(8):
        wx = float(gll_weights[x])
        robin = wx * (side_y + side_z)
        inv = inv_yz
        if x == 0:
            robin = robin + line(0) * w_yz
            inv = jnp.where(x_lo, 0.5 * inv_yz, inv_yz)
        if x == 7:
            robin = robin + line(1) * w_yz
            inv = jnp.where(x_hi, 0.5 * inv_yz, inv_yz)
        put(mass, x, (mass_coef * wx) * w_yz + robin)
        put(im, x, inv)
        put(wk, x, (wx * w_yz) * cond[x])
    for t in range(nt):
        for y in range(8):
            wkt[t, at(y), :] = wk.at[t][across(y), :]

    bf = jnp.bfloat16

    def pieces(v):
        h1 = v.astype(bf)
        rest = v - h1.astype(f32)
        h2 = rest.astype(bf)
        h3 = (rest - h2.astype(f32)).astype(bf)
        return jnp.concatenate([h1, h2], axis=1), jnp.concatenate([h3, h1], axis=1)

    def along_z(v, i):
        first, second = pieces(v)
        one = jnp.dot(first, mats[i, 0], preferred_element_type=f32)
        two = jnp.dot(second, mats[i, 1, :, 0:128], preferred_element_type=f32)
        return one[:, 0:128] + (one[:, 128:256] + two)

    def apply_local(s, k):
        rows = 64 * nt
        grad_z = along_z(vec[s].reshape(rows, 128), 0)
        back_z = along_z(wk[...].reshape(rows, 128) * grad_z, 1)
        for t, c in enumerate(chunks):
            turned = [vec.at[s, t][across(y), :] for y in range(8)]
            grad = along_planes(turned, D)
            back = along_planes([wkt[t, at(y), :] * grad[y] for y in range(8)], D.T)
            for y in range(8):
                tmp.at[t][across(y), :] = back[y]
            v = [vec[s, t, at(x), :] for x in range(8)]
            grad = along_planes(v, D)
            flux = [
                wk[t, at(x), :] * grad[x]
                - (scan_speed * float(gll_weights[x])) * (w_yz[:, c] * v[x])
                for x in range(8)
            ]
            back = along_planes(flux, D.T)
            for x in range(8):
                tmp[t, at(x), :] = tmp[t, at(x), :] + (mass[t, at(x), :] * v[x] + back[x])
        for x in range(8):
            side = jnp.concatenate(
                [back_z[64 * t + 8 * x : 64 * t + 8 * x + 8] for t in range(nt)], axis=1
            )
            put(loc.at[k], x, zfold(get(tmp, x) + side))

    parts[...] = jnp.zeros(parts.shape, f32)
    ones = jnp.ones((8, 128), f32)

    def put_dot(j, d, left, right):
        total = sum(left[x] * right[x] for x in range(8))
        parts[j, 8 * d : 8 * d + 8, :] = sum(total[:, c] for c in chunks)

    def planes_of(s):
        return [get(vec.at[s], x) for x in range(8)]

    def weighted(v):
        return [get(im, x) * v[x] for x in range(8)]

    def sum_start(j):
        rows = lax.dot_general(
            ones, parts[j], (((1,), (1,)), ((), ())),
            precision=HIGHEST, preferred_element_type=f32,
        )
        msg1[j] = rows[0:1]
        buf1[j, pl.ds(gx, 1)] = rows[0:1].reshape(1, 1, 128)
        for k in order_x:
            pltpu.make_async_remote_copy(
                src_ref=msg1.at[j], dst_ref=buf1.at[j, gx], send_sem=send_1,
                recv_sem=recv_1.at[j], device_id=(at_x(k), gy), device_id_type=MESH,
            ).start()

    def sum_middle(j):
        pltpu.make_async_copy(
            buf1.at[j, pl.ds(0, nx - 1)], buf1.at[j, pl.ds(0, nx - 1)], recv_1.at[j]
        ).wait()
        total = jnp.sum(buf1[j], axis=0)
        msg2[j] = total
        buf2[j, pl.ds(gy, 1)] = total.reshape(1, 1, 128)
        for k in order_y:
            pltpu.make_async_remote_copy(
                src_ref=msg2.at[j], dst_ref=buf2.at[j, gy], send_sem=send_2,
                recv_sem=recv_2.at[j], device_id=(gx, at_y(k)), device_id_type=MESH,
            ).start()

    pick = (
        lax.broadcasted_iota(jnp.int32, (16, 128), 1) // 8
        == lax.broadcasted_iota(jnp.int32, (16, 128), 0)
    )

    def sum_finish(j):
        pltpu.make_async_copy(
            buf2.at[j, pl.ds(0, ny - 1)], buf2.at[j, pl.ds(0, ny - 1)], recv_2.at[j]
        ).wait()
        total = jnp.broadcast_to(jnp.sum(buf2[j], axis=0), (16, 128))
        spread_rows = jnp.where(pick, total, 0.0)
        return jnp.dot(
            spread_rows, jnp.ones((128, 128), f32), precision=HIGHEST,
            preferred_element_type=f32,
        )

    def wide_of(scalar):
        return jnp.broadcast_to(jnp.concatenate([scalar] * len(chunks), axis=1), (8, nz))

    B, V1, V2, V3, V4, R, RA, RA2, RA3, PP, PA, PA2, PA3, PA4, X = range(15)

    halo_finish(0, B)
    apply_local(B, 1)
    halo_start(1)
    b = planes_of(B)
    bw = weighted(b)
    put_dot(0, 0, bw, b)
    halo_finish(1, V1)
    apply_local(V1, 2)
    halo_start(2)
    v1 = planes_of(V1)
    put_dot(0, 1, weighted(planes_of(B)), v1)
    put_dot(0, 2, weighted(v1), v1)
    halo_finish(2, V2)
    apply_local(V2, 3)
    halo_start(3)
    v2 = planes_of(V2)
    v2w = weighted(v2)
    put_dot(0, 3, v2w, planes_of(B))
    put_dot(0, 4, v2w, planes_of(V1))
    put_dot(0, 5, v2w, v2)
    sum_start(0)
    sum_middle(0)
    halo_finish(3, V3)
    apply_local(V3, 4)
    halo_start(4)
    halo_finish(4, V4)

    s = sum_finish(0)
    bb, bv1, v1v1, bv2, v1v2, v2v2 = [s[i : i + 1] for i in range(6)]
    rho = bb
    alpha = rho / bv1
    cross = bv1 - alpha * (v1v1 + bv2) + alpha * alpha * v1v2
    square = v1v1 - 2.0 * alpha * v1v2 + alpha * alpha * v2v2
    omega = cross / square
    rho_next = -omega * (bv1 - alpha * bv2)
    beta = rho_next / rho * (alpha / omega)
    rho = rho_next
    al, om, be = wide_of(alpha), wide_of(omega), wide_of(beta)
    for x in range(8):
        b, v1, v2, v3, v4 = [get(vec.at[i], x) for i in (B, V1, V2, V3, V4)]
        s0 = b - al * v1
        s1 = v1 - al * v2
        s2 = v2 - al * v3
        s3 = v3 - al * v4
        put(vec.at[X], x, al * b + om * s0)
        r0 = s0 - om * s1
        r1 = s1 - om * s2
        r2 = s2 - om * s3
        put(vec.at[R], x, r0)
        put(vec.at[RA], x, r1)
        put(vec.at[RA2], x, r2)
        put(vec.at[PP], x, r0 + be * (b - om * v1))
        put(vec.at[PA], x, r1 + be * (v1 - om * v2))
        put(vec.at[PA2], x, r2 + be * (v2 - om * v3))

    def put_dots(j):
        ra = planes_of(RA)
        raw = weighted(ra)
        put_dot(j, 0, raw, planes_of(R))
        put_dot(j, 1, raw, planes_of(PA))
        put_dot(j, 2, raw, ra)
        pa2 = planes_of(PA2)
        pa2w = weighted(pa2)
        put_dot(j, 3, pa2w, planes_of(R))
        put_dot(j, 4, pa2w, planes_of(PA))
        put_dot(j, 5, pa2w, ra)
        put_dot(j, 6, pa2w, pa2)
        bw = weighted(planes_of(B))
        put_dot(j, 7, bw, planes_of(PA))
        if j == 1:
            put_dot(j, 8, bw, ra)
            put_dot(j, 9, bw, pa2)

    def steps(j, rho):
        s = sum_finish(j)
        (ra_r, ra_pa, ra_ra, p2_r, p2_pa, p2_ra, p2_p2, b_pa, b_ra, b_p2) = [
            s[i : i + 1] for i in range(10)
        ]
        alpha = rho / b_pa
        cross = ra_r - alpha * (ra_pa + p2_r) + alpha * alpha * p2_pa
        square = ra_ra - 2.0 * alpha * p2_ra + alpha * alpha * p2_p2
        omega = cross / square
        rho_next = -omega * (b_ra - alpha * b_p2)
        beta = rho_next / rho * (alpha / omega)
        return alpha, omega, beta, rho_next

    apply_local(PA2, 5)
    halo_start(5)
    put_dots(1)
    sum_start(1)
    sum_middle(1)
    halo_finish(5, PA3)
    apply_local(PA3, 6)
    halo_start(6)
    for x in range(8):
        put(vec.at[RA3], x, get(vec.at[PA3], x) - be * (get(vec.at[V3], x) - om * get(vec.at[V4], x)))
    halo_finish(6, PA4)

    alpha, omega, beta, rho = steps(1, rho)
    al, om, be = wide_of(alpha), wide_of(omega), wide_of(beta)
    for x in range(8):
        r0, r1, r2, r3 = [get(vec.at[i], x) for i in (R, RA, RA2, RA3)]
        p0, p1, p2, p3, p4 = [get(vec.at[i], x) for i in (PP, PA, PA2, PA3, PA4)]
        s0 = r0 - al * p1
        s1 = r1 - al * p2
        s2 = r2 - al * p3
        s3 = r3 - al * p4
        put(vec.at[X], x, get(vec.at[X], x) + al * p0 + om * s0)
        r0 = s0 - om * s1
        r1 = s1 - om * s2
        r2 = s2 - om * s3
        put(vec.at[R], x, r0)
        put(vec.at[RA], x, r1)
        put(vec.at[PP], x, r0 + be * (p0 - om * p1))
        put(vec.at[PA], x, r1 + be * (p1 - om * p2))
        put(vec.at[PA2], x, r2 + be * (p2 - om * p3))

    put_dots(2)
    sum_start(2)
    sum_middle(2)
    alpha, omega, _, _ = steps(2, rho)
    al, om = wide_of(alpha), wide_of(omega)
    for x in range(8):
        s0 = get(vec.at[R], x) - al * get(vec.at[PA], x)
        s1 = get(vec.at[RA], x) - al * get(vec.at[PA2], x)
        adj_ref[x] = get(vec.at[X], x) + al * get(vec.at[PP], x) + om * s0
        res_ref[x] = s0 - om * s1

    pltpu.make_async_copy(xr, xr, send_x).wait()
    pltpu.make_async_copy(yr, yr, send_y).wait()
    lines = cr.at[:, 0, :, pl.ds(0, 4), :]
    pltpu.make_async_copy(lines, lines, send_c).wait()
    sent_1 = buf1.at[:, pl.ds(0, nx - 1)]
    pltpu.make_async_copy(sent_1, sent_1, send_1).wait()
    sent_2 = buf2.at[:, pl.ds(0, ny - 1)]
    pltpu.make_async_copy(sent_2, sent_2, send_2).wait()


def constants(nz):
    w = np.array(gll_weights)
    wz = np.tile(w, nz // 8)
    node = np.arange(nz) % 8
    elem = np.arange(nz) // 8
    shared = ((node == 7) & (elem < nz // 8 - 1)) | ((node == 0) & (elem > 0))
    inv_z = np.where(shared, 0.5, 1.0)
    planes = np.stack(
        [
            w[:, None] * wz[None, :],
            np.broadcast_to(inv_z, (8, nz)),
            np.broadcast_to(w[:, None], (8, nz)),
            np.broadcast_to(wz, (8, nz)),
        ]
    ).astype(np.float32)
    mats = []
    for small in (D.T, D):
        rest = np.kron(np.eye(16), small).astype(np.float32)
        parts = []
        for _ in range(3):
            part = rest.astype(jnp.bfloat16)
            parts.append(part)
            rest = rest - part.astype(np.float32)
        d1, d2, d3 = parts
        both = np.concatenate([d1, d2], axis=1)
        last = np.concatenate([d1, d3], axis=0)
        mats.append(
            np.stack(
                [
                    np.concatenate([both, both], axis=0),
                    np.concatenate([last, np.zeros_like(last)], axis=1),
                ]
            )
        )
    return np.stack(mats), planes


def solution(mesh):
    nx, ny = mesh.shape["gx"], mesh.shape["gy"]

    def per_device(source, conductivity, robin_flags, htc_class, htc_table):
        nz = source.shape[2]
        ez = robin_flags.shape[2]
        mats, planes = constants(nz)
        any_spec = pl.BlockSpec(memory_space=pl.ANY)
        vm = pltpu.VMEM
        dma = pltpu.SemaphoreType.DMA
        field = (8, 8, nz)
        nt = nz // 128
        flat = (nt, 64, 128)
        return pl.pallas_call(
            functools.partial(kernel, nx, ny, nz),
            out_shape=(jax.ShapeDtypeStruct(field, f32), jax.ShapeDtypeStruct(field, f32)),
            in_specs=[any_spec] * 7,
            out_specs=(pl.BlockSpec(memory_space=pltpu.VMEM),) * 2,
            scratch_shapes=[
                vm(field, f32),
                vm(field, f32),
                vm(flat, f32),
                vm(flat, f32),
                vm((1, ez), jnp.int32),
                vm((1, ez), jnp.int32),
                pltpu.SMEM((1, 4), f32),
                vm((2, 2, 256, 256), jnp.bfloat16),
                vm((4, 8, nz), f32),
                vm(flat, f32),
                vm(flat, f32),
                vm((ROUNDS,) + flat, f32),
                vm((15,) + flat, f32),
                vm(flat, f32),
                vm((ROUNDS, 2, nt, 8, 128), f32),
                vm((ROUNDS, 2, nt, 8, 128), f32),
                vm((ROUNDS, 2, nt, 8, 128), f32),
                vm((ROUNDS, 2, nt, 8, 128), f32),
                vm((SUMS, 128, 128), f32),
                vm((SUMS, 1, 128), f32),
                vm((SUMS, 1, 128), f32),
                vm((SUMS, nx, 1, 128), f32),
                vm((SUMS, ny, 1, 128), f32),
                dma((7,)),
                dma,
                dma,
                dma,
                dma((ROUNDS,)),
                dma((ROUNDS,)),
                dma((ROUNDS,)),
                dma,
                dma,
                dma((SUMS,)),
                dma((SUMS,)),
            ],
            compiler_params=pltpu.CompilerParams(collective_id=0, has_side_effects=True),
        )(
            source,
            conductivity,
            robin_flags.reshape(1, ez),
            htc_class.reshape(1, ez),
            htc_table.reshape(1, 4),
            mats,
            planes,
        )

    return jax.shard_map(
        per_device,
        mesh=mesh,
        in_specs=(
            P("gx", "gy", None),
            P("gx", "gy", None),
            P("gx", "gy", None),
            P("gx", "gy", None),
            P(),
        ),
        out_specs=(P("gx", "gy", None), P("gx", "gy", None)),
        check_vma=False,
    )
```

```python
import functools

import jax
import jax.numpy as jnp
import numpy as np
from jax import lax
from jax.experimental import pallas as pl
from jax.experimental.pallas import tpu as pltpu
from jax.sharding import PartitionSpec as P

MESH = pl.DeviceIdType.MESH
HIGHEST = lax.Precision.HIGHEST
f32 = jnp.float32

gll_points = (
    -1.0,
    -0.8717401485096066,
    -0.5917001814331423,
    -0.2092992179024789,
    0.2092992179024789,
    0.5917001814331423,
    0.8717401485096066,
    1.0,
)
gll_weights = (
    0.03571428571428571,
    0.21070422714350603,
    0.3411226924835044,
    0.4124587946587038,
    0.4124587946587038,
    0.3411226924835044,
    0.21070422714350603,
    0.03571428571428571,
)
mass_coef = 0.2
scan_speed = 2.0
ROUNDS = 7
SUMS = 3


def derivative_matrix():
    points = np.array(gll_points)
    bary = np.array(
        [1.0 / np.prod([points[j] - points[m] for m in range(8) if m != j]) for j in range(8)]
    )
    d = np.zeros((8, 8))
    for a in range(8):
        for b in range(8):
            if a != b:
                d[a, b] = bary[b] / bary[a] / (points[a] - points[b])
        d[a, a] = -np.sum(d[a])
    return d


D = derivative_matrix()


def along_planes(planes, mat):
    even = [planes[b] + planes[7 - b] for b in range(4)]
    odd = [planes[b] - planes[7 - b] for b in range(4)]
    out = [None] * 8
    for a in range(4):
        p = sum(float(0.5 * (mat[a, b] + mat[a, 7 - b])) * even[b] for b in range(4))
        q = sum(float(0.5 * (mat[a, b] - mat[a, 7 - b])) * odd[b] for b in range(4))
        out[a] = p + q
        out[7 - a] = q - p
    return out


def ends(planes, mat):
    even = [planes[b] + planes[7 - b] for b in range(4)]
    odd = [planes[b] - planes[7 - b] for b in range(4)]
    p = sum(float(0.5 * (mat[0, b] + mat[0, 7 - b])) * even[b] for b in range(4))
    q = sum(float(0.5 * (mat[0, b] - mat[0, 7 - b])) * odd[b] for b in range(4))
    return p + q, q - p


def kernel(
    nx, ny, nz,
    src_hbm, cond_hbm, flags_hbm, class_hbm, table_hbm, mats_hbm, planes_hbm,
    x_out, pp_out, r_out, pa_out, ra_out, pa2_out, al_out, om_out,
    src, cond, w2, wk, wkt, flags, classes, table, mats, planes, mass, im,
    loc, vec, tmp, fx, fy, ywk, xr, yr, cr, ysend,
    parts, msg1, msg2, buf1, buf2,
    in_sem, send_x, send_y, send_c, recv_x, recv_y, recv_c,
    send_1, send_2, recv_1, recv_2,
):
    gx = lax.axis_index("gx")
    gy = lax.axis_index("gy")

    def at_x(k):
        return (gx + (k % nx)) & (nx - 1)

    def at_y(k):
        return (gy + (k % ny)) & (ny - 1)

    loads = [
        pltpu.make_async_copy(a, b, in_sem.at[i])
        for i, (a, b) in enumerate(
            [
                (src_hbm, src),
                (planes_hbm, planes),
                (cond_hbm, cond),
                (mats_hbm, mats),
                (flags_hbm, flags),
                (class_hbm, classes),
                (table_hbm, table),
            ]
        )
    ]
    for c in loads[:2]:
        c.start()

    barrier = pltpu.get_barrier_semaphore()
    order_x = sorted(range(1, nx), key=lambda k: abs(k - nx // 2))
    order_y = sorted(range(1, ny), key=lambda k: abs(k - ny // 2))
    peers = [(at_x(dx), at_y(dy)) for dx in (-1, 1) for dy in (-1, 1)]
    peers += [(gx, at_y(k)) for k in order_y] + [(at_x(k), gy) for k in order_x]
    for peer in peers:
        pl.semaphore_signal(barrier, inc=1, device_id=peer, device_id_type=MESH)
    for c in loads[2:]:
        c.start()

    lane = lax.broadcasted_iota(jnp.int32, (8, nz), 1)
    node_z = lax.rem(lane, 8)
    row = lax.broadcasted_iota(jnp.int32, (8, nz), 0)
    join_up = (node_z == 7) & (lane < nz - 1)
    join_dn = (node_z == 0) & (lane > 0)
    zero = jnp.zeros((8, nz), f32)
    x_lo, x_hi = gx > 0, gx < nx - 1
    y_lo, y_hi = gy > 0, gy < ny - 1
    row_t = lax.broadcasted_iota(jnp.int32, (8, 128), 0)
    corner = ((row_t == 0) & x_lo) | ((row_t == 7) & x_hi)
    tile0 = jnp.zeros((8, 128), f32)
    chunks = [slice(128 * t, 128 * t + 128) for t in range(nz // 128)]

    def zfold(plane):
        up = pltpu.roll(plane, nz - 1, 1)
        dn = pltpu.roll(plane, 1, 1)
        return plane + jnp.where(join_up, up, jnp.where(join_dn, dn, zero))

    nt = len(chunks)

    def at(x):
        return slice(8 * x, 8 * x + 8)

    def get(ref, x):
        return jnp.concatenate([ref[t, at(x), :] for t in range(nt)], axis=1)

    def put(ref, x, plane):
        for t, c in enumerate(chunks):
            ref[t, at(x), :] = plane[:, c]

    def across(y):
        return pl.ds(y, 8, stride=8)

    for c in loads[:2]:
        c.wait()
    w_yz = planes[0]
    inv_z = planes[1]

    def send(s, d, ss, rs, peer):
        pltpu.make_async_remote_copy(
            src_ref=s, dst_ref=d, send_sem=ss, recv_sem=rs,
            device_id=peer, device_id_type=MESH,
        ).start()

    def y_start(k):
        for dx, dy in ((-1, -1), (-1, 1), (1, -1), (1, 1)):
            send(
                ysend.at[k, int(dy > 0), :, pl.ds(7 * (dx > 0), 1), :],
                cr.at[k, int(dy < 0), :, pl.ds(7 * (dx < 0), 1), :],
                send_c, recv_c.at[k], (at_x(dx), at_y(dy)),
            )
        for i, dy in enumerate((-1, 1)):
            send(ysend.at[k, i], yr.at[k, 1 - i], send_y, recv_y.at[k], (gx, at_y(dy)))

    def x_start(k):
        for i, dx in enumerate((-1, 1)):
            send(
                loc.at[k, :, pl.ds(56 * i, 8), :], xr.at[k, 1 - i],
                send_x, recv_x.at[k], (at_x(dx), gy),
            )

    def halo_finish(k, dst):
        for t in range(nt):
            vec[dst, t, 8:56, :] = loc[k, t, 8:56, :]
        pltpu.make_async_copy(xr.at[k], xr.at[k], recv_x.at[k]).wait()
        for t in range(nt):
            vec[dst, t, at(0), :] = loc[k, t, at(0), :] + jnp.where(x_lo, xr[k, 0, t], tile0)
            vec[dst, t, at(7), :] = loc[k, t, at(7), :] + jnp.where(x_hi, xr[k, 1, t], tile0)
        pltpu.make_async_copy(yr.at[k], yr.at[k], recv_y.at[k]).wait()
        lines = cr.at[k, 0, :, pl.ds(0, 4), :]
        pltpu.make_async_copy(lines, lines, recv_c.at[k]).wait()
        for i, has in enumerate((y_lo, y_hi)):
            for t in range(nt):
                add = yr[k, i, t] + jnp.where(corner, cr[k, i, t], tile0)
                add = jnp.where(has, add, tile0)
                vec.at[dst, t][across(7 * i), :] = vec.at[dst, t][across(7 * i), :] + add

    for x in range(8):
        put(loc.at[0], x, zfold(float(gll_weights[x]) * w_yz * src[x]))

    for i in (0, 1):
        for t in range(nt):
            ysend[0, i, t] = loc.at[0, t][across(7 * i), :]
    pl.semaphore_wait(barrier, len(peers))
    y_start(0)
    x_start(0)

    for c in loads[2:]:
        c.wait()
    bits = flags[...]
    kinds = classes[...]
    coef = jnp.zeros(kinds.shape, f32)
    for i in range(4):
        coef = coef + jnp.where(kinds == i, table[0, i], 0.0)
    edge = [gx == 0, gx == nx - 1, gy == 0, gy == ny - 1]
    faces = []
    for i in range(6):
        bit = lax.bitwise_and(lax.shift_right_logical(bits, i), 1).astype(f32)
        face = coef * bit
        if i < 4:
            face = jnp.where(edge[i], face, 0.0)
        faces.append(face)
    faces = jnp.concatenate(faces + [jnp.zeros((2, kinds.shape[1]), f32)], axis=0)
    elem = lax.broadcasted_iota(jnp.int32, (kinds.shape[1], nz), 0)
    spread = (lax.broadcasted_iota(jnp.int32, (kinds.shape[1], nz), 1) // 8 == elem).astype(f32)
    wide = jnp.dot(faces, spread, precision=HIGHEST, preferred_element_type=f32)

    def line(i):
        return jnp.broadcast_to(wide[i : i + 1], (8, nz))

    w_y = planes[2]
    w_z = planes[3]
    side_y = jnp.where(row == 0, line(2), jnp.where(row == 7, line(3), zero)) * w_z
    side_z = jnp.where(lane == 0, line(4), jnp.where(lane == nz - 1, line(5), zero)) * w_y
    inv_y = jnp.where(((row == 0) & y_lo) | ((row == 7) & y_hi), 0.5, 1.0).astype(f32)
    inv_yz = inv_y * inv_z
    for x in range(8):
        wx = float(gll_weights[x])
        robin = wx * (side_y + side_z)
        inv = inv_yz
        if x == 0:
            robin = robin + line(0) * w_yz
            inv = jnp.where(x_lo, 0.5 * inv_yz, inv_yz)
        if x == 7:
            robin = robin + line(1) * w_yz
            inv = jnp.where(x_hi, 0.5 * inv_yz, inv_yz)
        put(mass, x, (mass_coef * wx) * w_yz + robin)
        put(im, x, inv)
        w2[x] = (scan_speed * wx) * w_yz
        put(wk, x, (wx * w_yz) * cond[x])
    for t in range(nt):
        for y in range(8):
            wkt[t, at(y), :] = wk.at[t][across(y), :]
        for i in (0, 1):
            ywk[pl.ds(8 * (i * nt + t), 8), :] = wk.at[t][across(7 * i), :]

    bf = jnp.bfloat16

    def pieces(v):
        h1 = v.astype(bf)
        rest = v - h1.astype(f32)
        h2 = rest.astype(bf)
        h3 = (rest - h2.astype(f32)).astype(bf)
        return jnp.concatenate([h1, h2], axis=1), jnp.concatenate([h3, h1], axis=1)

    def along_z(v, i):
        first, second = pieces(v)
        one = jnp.dot(first, mats[i, 0], preferred_element_type=f32)
        two = jnp.dot(second, mats[i, 1, :, 0:128], preferred_element_type=f32)
        return one[:, 0:128] + (one[:, 128:256] + two)

    def apply_edges(s, k):
        rows = jnp.concatenate(
            [vec.at[s, t][across(7 * i), :] for i in (0, 1) for t in range(nt)], axis=0
        )
        face_z = along_z(ywk[...] * along_z(rows, 0), 1)
        face_y = [[], []]
        for t in range(nt):
            turned = [vec.at[s, t][across(y), :] for y in range(8)]
            grad = along_planes(turned, D)
            flux = [wkt[t, at(y), :] * grad[y] for y in range(8)]
            for y in range(8):
                fy[t, at(y), :] = flux[y]
            for i, end in enumerate(ends(flux, D.T)):
                face_y[i].append(end)
            v = [vec[s, t, at(x), :] for x in range(8)]
            grad = along_planes(v, D)
            flux = [wk[t, at(x), :] * grad[x] - w2[x, :, chunks[t]] * v[x] for x in range(8)]
            back = along_planes(flux, D.T)
            for x in range(8):
                fx[t, at(x), :] = mass[t, at(x), :] * v[x] + back[x]
        for i in (0, 1):
            face = [
                fx.at[t][across(7 * i), :]
                + face_y[i][t]
                + face_z[8 * (i * nt + t) : 8 * (i * nt + t) + 8]
                for t in range(nt)
            ]
            face = zfold(jnp.concatenate(face, axis=1))
            for t, c in enumerate(chunks):
                ysend[k, i, t] = face[:, c]
        y_start(k)

    def apply_rest(s, k):
        grad_z = along_z(vec[s].reshape(64 * nt, 128), 0)
        back_z = along_z(wk[...].reshape(64 * nt, 128) * grad_z, 1)
        for t in range(nt):
            back = along_planes([fy[t, at(y), :] for y in range(8)], D.T)
            for y in range(8):
                tmp.at[t][across(y), :] = back[y]
        for x in range(8):
            side = jnp.concatenate(
                [back_z[64 * t + 8 * x : 64 * t + 8 * x + 8] for t in range(nt)], axis=1
            )
            put(loc.at[k], x, zfold(get(tmp, x) + get(fx, x) + side))
        x_start(k)

    parts[...] = jnp.zeros(parts.shape, f32)
    ones = jnp.ones((8, 128), f32)

    def put_dot(j, d, left, right):
        total = sum(left[x] * right[x] for x in range(8))
        parts[j, 8 * d : 8 * d + 8, :] = sum(total[:, c] for c in chunks)

    def planes_of(s):
        return [get(vec.at[s], x) for x in range(8)]

    def weighted(v):
        return [get(im, x) * v[x] for x in range(8)]

    def sum_start(j):
        rows = lax.dot_general(
            ones, parts[j], (((1,), (1,)), ((), ())),
            precision=HIGHEST, preferred_element_type=f32,
        )
        msg1[j] = rows[0:1]
        buf1[j, pl.ds(gx, 1)] = rows[0:1].reshape(1, 1, 128)
        for k in order_x:
            pltpu.make_async_remote_copy(
                src_ref=msg1.at[j], dst_ref=buf1.at[j, gx], send_sem=send_1,
                recv_sem=recv_1.at[j], device_id=(at_x(k), gy), device_id_type=MESH,
            ).start()

    def sum_middle(j):
        pltpu.make_async_copy(
            buf1.at[j, pl.ds(0, nx - 1)], buf1.at[j, pl.ds(0, nx - 1)], recv_1.at[j]
        ).wait()
        total = jnp.sum(buf1[j], axis=0)
        msg2[j] = total
        buf2[j, pl.ds(gy, 1)] = total.reshape(1, 1, 128)
        for k in order_y:
            pltpu.make_async_remote_copy(
                src_ref=msg2.at[j], dst_ref=buf2.at[j, gy], send_sem=send_2,
                recv_sem=recv_2.at[j], device_id=(gx, at_y(k)), device_id_type=MESH,
            ).start()

    pick = (
        lax.broadcasted_iota(jnp.int32, (16, 128), 1) // 8
        == lax.broadcasted_iota(jnp.int32, (16, 128), 0)
    )

    def sum_finish(j):
        pltpu.make_async_copy(
            buf2.at[j, pl.ds(0, ny - 1)], buf2.at[j, pl.ds(0, ny - 1)], recv_2.at[j]
        ).wait()
        total = jnp.broadcast_to(jnp.sum(buf2[j], axis=0), (16, 128))
        spread_rows = jnp.where(pick, total, 0.0)
        return jnp.dot(
            spread_rows, jnp.ones((128, 128), f32), precision=HIGHEST,
            preferred_element_type=f32,
        )

    def wide_of(scalar):
        return jnp.broadcast_to(jnp.concatenate([scalar] * len(chunks), axis=1), (8, nz))

    B, V1, V2, V3, V4, R, RA, RA2, RA3, PP, PA, PA2, PA3, PA4, X, NR, NPA = range(17)

    halo_finish(0, B)
    apply_edges(B, 1)
    apply_rest(B, 1)
    b = planes_of(B)
    bw = weighted(b)
    put_dot(0, 0, bw, b)
    halo_finish(1, V1)
    apply_edges(V1, 2)
    apply_rest(V1, 2)
    v1 = planes_of(V1)
    put_dot(0, 1, weighted(planes_of(B)), v1)
    put_dot(0, 2, weighted(v1), v1)
    halo_finish(2, V2)
    apply_edges(V2, 3)
    v2 = planes_of(V2)
    v2w = weighted(v2)
    put_dot(0, 3, v2w, planes_of(B))
    put_dot(0, 4, v2w, planes_of(V1))
    put_dot(0, 5, v2w, v2)
    sum_start(0)
    apply_rest(V2, 3)
    sum_middle(0)
    halo_finish(3, V3)
    apply_edges(V3, 4)
    apply_rest(V3, 4)
    halo_finish(4, V4)

    s = sum_finish(0)
    bb, bv1, v1v1, bv2, v1v2, v2v2 = [s[i : i + 1] for i in range(6)]
    rho = bb
    alpha = rho / bv1
    cross = bv1 - alpha * (v1v1 + bv2) + alpha * alpha * v1v2
    square = v1v1 - 2.0 * alpha * v1v2 + alpha * alpha * v2v2
    omega = cross / square
    rho_next = -omega * (bv1 - alpha * bv2)
    beta = rho_next / rho * (alpha / omega)
    rho = rho_next
    al, om, be = wide_of(alpha), wide_of(omega), wide_of(beta)
    for x in range(8):
        v2, v3, v4 = [get(vec.at[i], x) for i in (V2, V3, V4)]
        s2 = v2 - al * v3
        r2 = s2 - om * (v3 - al * v4)
        put(vec.at[RA2], x, r2)
        put(vec.at[PA2], x, r2 + be * (v2 - om * v3))
    apply_edges(PA2, 5)
    for x in range(8):
        b, v1, v2, v3 = [get(vec.at[i], x) for i in (B, V1, V2, V3)]
        s0 = b - al * v1
        s1 = v1 - al * v2
        put(vec.at[X], x, al * b + om * s0)
        r0 = s0 - om * s1
        r1 = s1 - om * (v2 - al * v3)
        put(vec.at[R], x, r0)
        put(vec.at[RA], x, r1)
        put(vec.at[PP], x, r0 + be * (b - om * v1))
        put(vec.at[PA], x, r1 + be * (v1 - om * v2))

    def put_dots(j):
        r_slot, pa_slot = (R, PA) if j == 1 else (NR, NPA)
        ra = planes_of(RA)
        raw = weighted(ra)
        put_dot(j, 0, raw, planes_of(r_slot))
        put_dot(j, 1, raw, planes_of(pa_slot))
        put_dot(j, 2, raw, ra)
        pa2 = planes_of(PA2)
        pa2w = weighted(pa2)
        put_dot(j, 3, pa2w, planes_of(r_slot))
        put_dot(j, 4, pa2w, planes_of(pa_slot))
        put_dot(j, 5, pa2w, ra)
        put_dot(j, 6, pa2w, pa2)
        bw = weighted(planes_of(B))
        put_dot(j, 7, bw, planes_of(pa_slot))
        if j == 1:
            put_dot(j, 8, bw, ra)
            put_dot(j, 9, bw, pa2)

    def steps(j, rho):
        s = sum_finish(j)
        (ra_r, ra_pa, ra_ra, p2_r, p2_pa, p2_ra, p2_p2, b_pa, b_ra, b_p2) = [
            s[i : i + 1] for i in range(10)
        ]
        alpha = rho / b_pa
        cross = ra_r - alpha * (ra_pa + p2_r) + alpha * alpha * p2_pa
        square = ra_ra - 2.0 * alpha * p2_ra + alpha * alpha * p2_p2
        omega = cross / square
        rho_next = -omega * (b_ra - alpha * b_p2)
        beta = rho_next / rho * (alpha / omega)
        return alpha, omega, beta, rho_next

    put_dots(1)
    sum_start(1)
    apply_rest(PA2, 5)
    sum_middle(1)
    halo_finish(5, PA3)
    apply_edges(PA3, 6)
    apply_rest(PA3, 6)
    for x in range(8):
        put(vec.at[RA3], x, get(vec.at[PA3], x) - be * (get(vec.at[V3], x) - om * get(vec.at[V4], x)))
    halo_finish(6, PA4)

    alpha, omega, beta, rho = steps(1, rho)
    al, om, be = wide_of(alpha), wide_of(omega), wide_of(beta)
    for x in range(8):
        r0, r1, r2, r3 = [get(vec.at[i], x) for i in (R, RA, RA2, RA3)]
        p0, p1, p2, p3, p4 = [get(vec.at[i], x) for i in (PP, PA, PA2, PA3, PA4)]
        s0 = r0 - al * p1
        s1 = r1 - al * p2
        s2 = r2 - al * p3
        s3 = r3 - al * p4
        r0 = s0 - om * s1
        r1 = s1 - om * s2
        r2 = s2 - om * s3
        put(vec.at[NR], x, r0)
        put(vec.at[RA], x, r1)
        put(vec.at[NPA], x, r1 + be * (p1 - om * p2))
        put(vec.at[PA2], x, r2 + be * (p2 - om * p3))

    put_dots(2)
    sum_start(2)
    for x in range(8):
        r, p0, p1, r0 = [get(vec.at[i], x) for i in (R, PP, PA, NR)]
        x_out[x] = get(vec.at[X], x) + al * p0 + om * (r - al * p1)
        pp_out[x] = r0 + be * (p0 - om * p1)
        r_out[x] = r0
        pa_out[x] = get(vec.at[NPA], x)
        ra_out[x] = get(vec.at[RA], x)
        pa2_out[x] = get(vec.at[PA2], x)
    sum_middle(2)
    alpha, omega, _, _ = steps(2, rho)
    al_out[...] = wide_of(alpha)
    om_out[...] = wide_of(omega)

    pltpu.make_async_copy(xr, xr, send_x).wait()
    pltpu.make_async_copy(yr, yr, send_y).wait()
    lines = cr.at[:, 0, :, pl.ds(0, 4), :]
    pltpu.make_async_copy(lines, lines, send_c).wait()
    sent_1 = buf1.at[:, pl.ds(0, nx - 1)]
    pltpu.make_async_copy(sent_1, sent_1, send_1).wait()
    sent_2 = buf2.at[:, pl.ds(0, ny - 1)]
    pltpu.make_async_copy(sent_2, sent_2, send_2).wait()


def constants(nz):
    w = np.array(gll_weights)
    wz = np.tile(w, nz // 8)
    node = np.arange(nz) % 8
    elem = np.arange(nz) // 8
    shared = ((node == 7) & (elem < nz // 8 - 1)) | ((node == 0) & (elem > 0))
    inv_z = np.where(shared, 0.5, 1.0)
    planes = np.stack(
        [
            w[:, None] * wz[None, :],
            np.broadcast_to(inv_z, (8, nz)),
            np.broadcast_to(w[:, None], (8, nz)),
            np.broadcast_to(wz, (8, nz)),
        ]
    ).astype(np.float32)
    mats = []
    for small in (D.T, D):
        rest = np.kron(np.eye(16), small).astype(np.float32)
        parts = []
        for _ in range(3):
            part = rest.astype(jnp.bfloat16)
            parts.append(part)
            rest = rest - part.astype(np.float32)
        d1, d2, d3 = parts
        both = np.concatenate([d1, d2], axis=1)
        last = np.concatenate([d1, d3], axis=0)
        mats.append(
            np.stack(
                [
                    np.concatenate([both, both], axis=0),
                    np.concatenate([last, np.zeros_like(last)], axis=1),
                ]
            )
        )
    return np.stack(mats), planes


def solution(mesh):
    nx, ny = mesh.shape["gx"], mesh.shape["gy"]

    def per_device(source, conductivity, robin_flags, htc_class, htc_table):
        nz = source.shape[2]
        ez = robin_flags.shape[2]
        mats, planes = constants(nz)
        any_spec = pl.BlockSpec(memory_space=pl.ANY)
        vm = pltpu.VMEM
        dma = pltpu.SemaphoreType.DMA
        field = (8, 8, nz)
        nt = nz // 128
        flat = (nt, 64, 128)
        x, pp, r, pa, ra, pa2, alpha, omega = pl.pallas_call(
            functools.partial(kernel, nx, ny, nz),
            out_shape=(pltpu.VMEM(field, f32),) * 6 + (pltpu.VMEM((8, nz), f32),) * 2,
            in_specs=[any_spec] * 7,
            out_specs=(pl.BlockSpec(memory_space=pltpu.VMEM),) * 8,
            scratch_shapes=[
                vm(field, f32),
                vm(field, f32),
                vm(field, f32),
                vm(flat, f32),
                vm(flat, f32),
                vm((1, ez), jnp.int32),
                vm((1, ez), jnp.int32),
                pltpu.SMEM((1, 4), f32),
                vm((2, 2, 256, 256), jnp.bfloat16),
                vm((4, 8, nz), f32),
                vm(flat, f32),
                vm(flat, f32),
                vm((ROUNDS,) + flat, f32),
                vm((17,) + flat, f32),
                vm(flat, f32),
                vm(flat, f32),
                vm(flat, f32),
                vm((16 * nt, 128), f32),
                vm((ROUNDS, 2, nt, 8, 128), f32),
                vm((ROUNDS, 2, nt, 8, 128), f32),
                vm((ROUNDS, 2, nt, 8, 128), f32),
                vm((ROUNDS, 2, nt, 8, 128), f32),
                vm((SUMS, 128, 128), f32),
                vm((SUMS, 1, 128), f32),
                vm((SUMS, 1, 128), f32),
                vm((SUMS, nx, 1, 128), f32),
                vm((SUMS, ny, 1, 128), f32),
                dma((7,)),
                dma,
                dma,
                dma,
                dma((ROUNDS,)),
                dma((ROUNDS,)),
                dma((ROUNDS,)),
                dma,
                dma,
                dma((SUMS,)),
                dma((SUMS,)),
            ],
            compiler_params=pltpu.CompilerParams(collective_id=0, has_side_effects=True),
        )(
            source,
            conductivity,
            robin_flags.reshape(1, ez),
            htc_class.reshape(1, ez),
            htc_table.reshape(1, 4),
            mats,
            planes,
        )
        half = r - alpha * pa
        return x + alpha * pp + omega * half, half - omega * (ra - alpha * pa2)

    return jax.shard_map(
        per_device,
        mesh=mesh,
        in_specs=(
            P("gx", "gy", None),
            P("gx", "gy", None),
            P("gx", "gy", None),
            P("gx", "gy", None),
            P(),
        ),
        out_specs=(P("gx", "gy", None), P("gx", "gy", None)),
        check_vma=False,
    )
```

```python
import functools

import jax
import jax.numpy as jnp
import numpy as np
from jax import lax
from jax.experimental import pallas as pl
from jax.experimental.pallas import tpu as pltpu
from jax.sharding import PartitionSpec as P

MESH = pl.DeviceIdType.MESH
HIGHEST = lax.Precision.HIGHEST
f32 = jnp.float32

gll_points = (
    -1.0,
    -0.8717401485096066,
    -0.5917001814331423,
    -0.2092992179024789,
    0.2092992179024789,
    0.5917001814331423,
    0.8717401485096066,
    1.0,
)
gll_weights = (
    0.03571428571428571,
    0.21070422714350603,
    0.3411226924835044,
    0.4124587946587038,
    0.4124587946587038,
    0.3411226924835044,
    0.21070422714350603,
    0.03571428571428571,
)
mass_coef = 0.2
scan_speed = 2.0
ROUNDS = 7
SUMS = 3


def derivative_matrix():
    points = np.array(gll_points)
    bary = np.array(
        [1.0 / np.prod([points[j] - points[m] for m in range(8) if m != j]) for j in range(8)]
    )
    d = np.zeros((8, 8))
    for a in range(8):
        for b in range(8):
            if a != b:
                d[a, b] = bary[b] / bary[a] / (points[a] - points[b])
        d[a, a] = -np.sum(d[a])
    return d


D = derivative_matrix()


def along_planes(planes, mat):
    even = [planes[b] + planes[7 - b] for b in range(4)]
    odd = [planes[b] - planes[7 - b] for b in range(4)]
    out = [None] * 8
    for a in range(4):
        p = sum(float(0.5 * (mat[a, b] + mat[a, 7 - b])) * even[b] for b in range(4))
        q = sum(float(0.5 * (mat[a, b] - mat[a, 7 - b])) * odd[b] for b in range(4))
        out[a] = p + q
        out[7 - a] = q - p
    return out


def ends(planes, mat):
    even = [planes[b] + planes[7 - b] for b in range(4)]
    odd = [planes[b] - planes[7 - b] for b in range(4)]
    p = sum(float(0.5 * (mat[0, b] + mat[0, 7 - b])) * even[b] for b in range(4))
    q = sum(float(0.5 * (mat[0, b] - mat[0, 7 - b])) * odd[b] for b in range(4))
    return p + q, q - p


def kernel(
    nx, ny, nz,
    src_hbm, cond_hbm, flags_hbm, class_hbm, table_hbm, mats_hbm, planes_hbm,
    x_out, pp_out, r_out, pa_out, ra_out, pa2_out, al_out, om_out,
    src, rows, cond, w2, wk, wkt, flags, classes, table, mats, planes, mass, im,
    loc, vec, tmp, fx, fy, ywk, xr, yr, cr, ysend,
    parts, msg1, msg2, buf1, buf2,
    in_sem, send_x, send_y, send_c, recv_x, recv_y, recv_c,
    send_1, send_2, recv_1, recv_2,
):
    gx = lax.axis_index("gx")
    gy = lax.axis_index("gy")

    def at_x(k):
        return (gx + (k % nx)) & (nx - 1)

    def at_y(k):
        return (gy + (k % ny)) & (ny - 1)

    loads = [
        pltpu.make_async_copy(a, b, in_sem.at[i])
        for i, (a, b) in enumerate(
            [
                (src_hbm.at[:, 0, :], rows.at[0]),
                (src_hbm.at[:, 7, :], rows.at[1]),
                (src_hbm.at[0], src.at[0]),
                (src_hbm.at[7], src.at[7]),
                (planes_hbm, planes),
                (src_hbm.at[pl.ds(1, 6)], src.at[pl.ds(1, 6)]),
                (cond_hbm, cond),
                (mats_hbm, mats),
                (flags_hbm, flags),
                (class_hbm, classes),
                (table_hbm, table),
            ]
        )
    ]
    for c in loads[:6]:
        c.start()

    barrier = pltpu.get_barrier_semaphore()
    order_x = sorted(range(1, nx), key=lambda k: abs(k - nx // 2))
    order_y = sorted(range(1, ny), key=lambda k: abs(k - ny // 2))
    peers = [(at_x(dx), at_y(dy)) for dx in (-1, 1) for dy in (-1, 1)]
    peers += [(gx, at_y(k)) for k in order_y] + [(at_x(k), gy) for k in order_x]
    for peer in peers:
        pl.semaphore_signal(barrier, inc=1, device_id=peer, device_id_type=MESH)
    for c in loads[6:]:
        c.start()

    lane = lax.broadcasted_iota(jnp.int32, (8, nz), 1)
    node_z = lax.rem(lane, 8)
    row = lax.broadcasted_iota(jnp.int32, (8, nz), 0)
    join_up = (node_z == 7) & (lane < nz - 1)
    join_dn = (node_z == 0) & (lane > 0)
    zero = jnp.zeros((8, nz), f32)
    x_lo, x_hi = gx > 0, gx < nx - 1
    y_lo, y_hi = gy > 0, gy < ny - 1
    row_t = lax.broadcasted_iota(jnp.int32, (8, 128), 0)
    corner = ((row_t == 0) & x_lo) | ((row_t == 7) & x_hi)
    tile0 = jnp.zeros((8, 128), f32)
    chunks = [slice(128 * t, 128 * t + 128) for t in range(nz // 128)]

    def zfold(plane):
        up = pltpu.roll(plane, nz - 1, 1)
        dn = pltpu.roll(plane, 1, 1)
        return plane + jnp.where(join_up, up, jnp.where(join_dn, dn, zero))

    nt = len(chunks)

    def at(x):
        return slice(8 * x, 8 * x + 8)

    def get(ref, x):
        return jnp.concatenate([ref[t, at(x), :] for t in range(nt)], axis=1)

    def put(ref, x, plane):
        for t, c in enumerate(chunks):
            ref[t, at(x), :] = plane[:, c]

    def across(y):
        return pl.ds(y, 8, stride=8)

    for c in loads[:5]:
        c.wait()
    w_yz = planes[0]
    inv_z = planes[1]

    def send(s, d, ss, rs, peer):
        pltpu.make_async_remote_copy(
            src_ref=s, dst_ref=d, send_sem=ss, recv_sem=rs,
            device_id=peer, device_id_type=MESH,
        ).start()

    def y_start(k):
        for dx, dy in ((-1, -1), (-1, 1), (1, -1), (1, 1)):
            send(
                ysend.at[k, int(dy > 0), :, pl.ds(7 * (dx > 0), 1), :],
                cr.at[k, int(dy < 0), :, pl.ds(7 * (dx < 0), 1), :],
                send_c, recv_c.at[k], (at_x(dx), at_y(dy)),
            )
        for i, dy in enumerate((-1, 1)):
            send(ysend.at[k, i], yr.at[k, 1 - i], send_y, recv_y.at[k], (gx, at_y(dy)))

    def x_start(k):
        for i, dx in enumerate((-1, 1)):
            send(
                loc.at[k, :, pl.ds(56 * i, 8), :], xr.at[k, 1 - i],
                send_x, recv_x.at[k], (at_x(dx), gy),
            )

    def halo_finish(k, dst):
        for t in range(nt):
            vec[dst, t, 8:56, :] = loc[k, t, 8:56, :]
        pltpu.make_async_copy(xr.at[k], xr.at[k], recv_x.at[k]).wait()
        for t in range(nt):
            vec[dst, t, at(0), :] = loc[k, t, at(0), :] + jnp.where(x_lo, xr[k, 0, t], tile0)
            vec[dst, t, at(7), :] = loc[k, t, at(7), :] + jnp.where(x_hi, xr[k, 1, t], tile0)
        pltpu.make_async_copy(yr.at[k], yr.at[k], recv_y.at[k]).wait()
        lines = cr.at[k, 0, :, pl.ds(0, 4), :]
        pltpu.make_async_copy(lines, lines, recv_c.at[k]).wait()
        for i, has in enumerate((y_lo, y_hi)):
            for t in range(nt):
                add = yr[k, i, t] + jnp.where(corner, cr[k, i, t], tile0)
                add = jnp.where(has, add, tile0)
                vec.at[dst, t][across(7 * i), :] = vec.at[dst, t][across(7 * i), :] + add

    end = float(gll_weights[0])
    for i in (0, 1):
        face = zfold(end * w_yz * rows[i])
        for t, c in enumerate(chunks):
            ysend[0, i, t] = face[:, c]
        put(loc.at[0], 7 * i, zfold(end * w_yz * src[7 * i]))
    pl.semaphore_wait(barrier, len(peers))
    y_start(0)
    x_start(0)
    loads[5].wait()
    for x in range(1, 7):
        put(loc.at[0], x, zfold(float(gll_weights[x]) * w_yz * src[x]))

    for c in loads[6:]:
        c.wait()
    bits = flags[...]
    kinds = classes[...]
    coef = jnp.zeros(kinds.shape, f32)
    for i in range(4):
        coef = coef + jnp.where(kinds == i, table[0, i], 0.0)
    edge = [gx == 0, gx == nx - 1, gy == 0, gy == ny - 1]
    faces = []
    for i in range(6):
        bit = lax.bitwise_and(lax.shift_right_logical(bits, i), 1).astype(f32)
        face = coef * bit
        if i < 4:
            face = jnp.where(edge[i], face, 0.0)
        faces.append(face)
    faces = jnp.concatenate(faces + [jnp.zeros((2, kinds.shape[1]), f32)], axis=0)
    elem = lax.broadcasted_iota(jnp.int32, (kinds.shape[1], nz), 0)
    spread = (lax.broadcasted_iota(jnp.int32, (kinds.shape[1], nz), 1) // 8 == elem).astype(f32)
    wide = jnp.dot(faces, spread, precision=HIGHEST, preferred_element_type=f32)

    def line(i):
        return jnp.broadcast_to(wide[i : i + 1], (8, nz))

    w_y = planes[2]
    w_z = planes[3]
    side_y = jnp.where(row == 0, line(2), jnp.where(row == 7, line(3), zero)) * w_z
    side_z = jnp.where(lane == 0, line(4), jnp.where(lane == nz - 1, line(5), zero)) * w_y
    inv_y = jnp.where(((row == 0) & y_lo) | ((row == 7) & y_hi), 0.5, 1.0).astype(f32)
    inv_yz = inv_y * inv_z
    for x in range(8):
        wx = float(gll_weights[x])
        robin = wx * (side_y + side_z)
        inv = inv_yz
        if x == 0:
            robin = robin + line(0) * w_yz
            inv = jnp.where(x_lo, 0.5 * inv_yz, inv_yz)
        if x == 7:
            robin = robin + line(1) * w_yz
            inv = jnp.where(x_hi, 0.5 * inv_yz, inv_yz)
        put(mass, x, (mass_coef * wx) * w_yz + robin)
        put(im, x, inv)
        w2[x] = (scan_speed * wx) * w_yz
        put(wk, x, (wx * w_yz) * cond[x])
    for t in range(nt):
        for y in range(8):
            wkt[t, at(y), :] = wk.at[t][across(y), :]
        for i in (0, 1):
            ywk[pl.ds(8 * (i * nt + t), 8), :] = wk.at[t][across(7 * i), :]

    bf = jnp.bfloat16

    def pieces(v):
        h1 = v.astype(bf)
        rest = v - h1.astype(f32)
        h2 = rest.astype(bf)
        h3 = (rest - h2.astype(f32)).astype(bf)
        return jnp.concatenate([h1, h2], axis=1), jnp.concatenate([h3, h1], axis=1)

    def along_z(v, i):
        first, second = pieces(v)
        one = jnp.dot(first, mats[i, 0], preferred_element_type=f32)
        two = jnp.dot(second, mats[i, 1, :, 0:128], preferred_element_type=f32)
        return one[:, 0:128] + (one[:, 128:256] + two)

    def apply_edges(s, k):
        rows = jnp.concatenate(
            [vec.at[s, t][across(7 * i), :] for i in (0, 1) for t in range(nt)], axis=0
        )
        face_z = along_z(ywk[...] * along_z(rows, 0), 1)
        face_y = [[], []]
        for t in range(nt):
            turned = [vec.at[s, t][across(y), :] for y in range(8)]
            grad = along_planes(turned, D)
            flux = [wkt[t, at(y), :] * grad[y] for y in range(8)]
            for y in range(8):
                fy[t, at(y), :] = flux[y]
            for i, end in enumerate(ends(flux, D.T)):
                face_y[i].append(end)
            v = [vec[s, t, at(x), :] for x in range(8)]
            grad = along_planes(v, D)
            flux = [wk[t, at(x), :] * grad[x] - w2[x, :, chunks[t]] * v[x] for x in range(8)]
            back = along_planes(flux, D.T)
            for x in range(8):
                fx[t, at(x), :] = mass[t, at(x), :] * v[x] + back[x]
        for i in (0, 1):
            face = [
                fx.at[t][across(7 * i), :]
                + face_y[i][t]
                + face_z[8 * (i * nt + t) : 8 * (i * nt + t) + 8]
                for t in range(nt)
            ]
            face = zfold(jnp.concatenate(face, axis=1))
            for t, c in enumerate(chunks):
                ysend[k, i, t] = face[:, c]
        y_start(k)

    def apply_rest(s, k):
        grad_z = along_z(vec[s].reshape(64 * nt, 128), 0)
        back_z = along_z(wk[...].reshape(64 * nt, 128) * grad_z, 1)
        for t in range(nt):
            back = along_planes([fy[t, at(y), :] for y in range(8)], D.T)
            for y in range(8):
                tmp.at[t][across(y), :] = back[y]
        for x in range(8):
            side = jnp.concatenate(
                [back_z[64 * t + 8 * x : 64 * t + 8 * x + 8] for t in range(nt)], axis=1
            )
            put(loc.at[k], x, zfold(get(tmp, x) + get(fx, x) + side))
        x_start(k)

    parts[...] = jnp.zeros(parts.shape, f32)
    ones = jnp.ones((8, 128), f32)

    def put_dot(j, d, left, right):
        total = sum(left[x] * right[x] for x in range(8))
        parts[j, 8 * d : 8 * d + 8, :] = sum(total[:, c] for c in chunks)

    def planes_of(s):
        return [get(vec.at[s], x) for x in range(8)]

    def weighted(v):
        return [get(im, x) * v[x] for x in range(8)]

    def sum_start(j):
        rows = lax.dot_general(
            ones, parts[j], (((1,), (1,)), ((), ())),
            precision=HIGHEST, preferred_element_type=f32,
        )
        msg1[j] = rows[0:1]
        buf1[j, pl.ds(gx, 1)] = rows[0:1].reshape(1, 1, 128)
        for k in order_x:
            pltpu.make_async_remote_copy(
                src_ref=msg1.at[j], dst_ref=buf1.at[j, gx], send_sem=send_1,
                recv_sem=recv_1.at[j], device_id=(at_x(k), gy), device_id_type=MESH,
            ).start()

    def sum_middle(j):
        pltpu.make_async_copy(
            buf1.at[j, pl.ds(0, nx - 1)], buf1.at[j, pl.ds(0, nx - 1)], recv_1.at[j]
        ).wait()
        total = jnp.sum(buf1[j], axis=0)
        msg2[j] = total
        buf2[j, pl.ds(gy, 1)] = total.reshape(1, 1, 128)
        for k in order_y:
            pltpu.make_async_remote_copy(
                src_ref=msg2.at[j], dst_ref=buf2.at[j, gy], send_sem=send_2,
                recv_sem=recv_2.at[j], device_id=(gx, at_y(k)), device_id_type=MESH,
            ).start()

    pick = (
        lax.broadcasted_iota(jnp.int32, (16, 128), 1) // 8
        == lax.broadcasted_iota(jnp.int32, (16, 128), 0)
    )

    def sum_finish(j):
        pltpu.make_async_copy(
            buf2.at[j, pl.ds(0, ny - 1)], buf2.at[j, pl.ds(0, ny - 1)], recv_2.at[j]
        ).wait()
        total = jnp.broadcast_to(jnp.sum(buf2[j], axis=0), (16, 128))
        spread_rows = jnp.where(pick, total, 0.0)
        return jnp.dot(
            spread_rows, jnp.ones((128, 128), f32), precision=HIGHEST,
            preferred_element_type=f32,
        )

    def wide_of(scalar):
        return jnp.broadcast_to(jnp.concatenate([scalar] * len(chunks), axis=1), (8, nz))

    B, V1, V2, V3, V4, R, RA, RA2, RA3, PP, PA, PA2, PA3, PA4, X, NR, NPA = range(17)

    halo_finish(0, B)
    apply_edges(B, 1)
    apply_rest(B, 1)
    b = planes_of(B)
    bw = weighted(b)
    put_dot(0, 0, bw, b)
    halo_finish(1, V1)
    apply_edges(V1, 2)
    apply_rest(V1, 2)
    v1 = planes_of(V1)
    put_dot(0, 1, weighted(planes_of(B)), v1)
    put_dot(0, 2, weighted(v1), v1)
    halo_finish(2, V2)
    apply_edges(V2, 3)
    v2 = planes_of(V2)
    v2w = weighted(v2)
    put_dot(0, 3, v2w, planes_of(B))
    put_dot(0, 4, v2w, planes_of(V1))
    put_dot(0, 5, v2w, v2)
    sum_start(0)
    apply_rest(V2, 3)
    sum_middle(0)
    halo_finish(3, V3)
    apply_edges(V3, 4)
    apply_rest(V3, 4)
    halo_finish(4, V4)

    s = sum_finish(0)
    bb, bv1, v1v1, bv2, v1v2, v2v2 = [s[i : i + 1] for i in range(6)]
    rho = bb
    alpha = rho / bv1
    cross = bv1 - alpha * (v1v1 + bv2) + alpha * alpha * v1v2
    square = v1v1 - 2.0 * alpha * v1v2 + alpha * alpha * v2v2
    omega = cross / square
    rho_next = -omega * (bv1 - alpha * bv2)
    beta = rho_next / rho * (alpha / omega)
    rho = rho_next
    al, om, be = wide_of(alpha), wide_of(omega), wide_of(beta)
    for x in range(8):
        v2, v3, v4 = [get(vec.at[i], x) for i in (V2, V3, V4)]
        s2 = v2 - al * v3
        r2 = s2 - om * (v3 - al * v4)
        put(vec.at[RA2], x, r2)
        put(vec.at[PA2], x, r2 + be * (v2 - om * v3))
    apply_edges(PA2, 5)
    for x in range(8):
        b, v1, v2, v3 = [get(vec.at[i], x) for i in (B, V1, V2, V3)]
        s0 = b - al * v1
        s1 = v1 - al * v2
        put(vec.at[X], x, al * b + om * s0)
        r0 = s0 - om * s1
        r1 = s1 - om * (v2 - al * v3)
        put(vec.at[R], x, r0)
        put(vec.at[RA], x, r1)
        put(vec.at[PP], x, r0 + be * (b - om * v1))
        put(vec.at[PA], x, r1 + be * (v1 - om * v2))

    def put_dots(j):
        r_slot, pa_slot = (R, PA) if j == 1 else (NR, NPA)
        ra = planes_of(RA)
        raw = weighted(ra)
        put_dot(j, 0, raw, planes_of(r_slot))
        put_dot(j, 1, raw, planes_of(pa_slot))
        put_dot(j, 2, raw, ra)
        pa2 = planes_of(PA2)
        pa2w = weighted(pa2)
        put_dot(j, 3, pa2w, planes_of(r_slot))
        put_dot(j, 4, pa2w, planes_of(pa_slot))
        put_dot(j, 5, pa2w, ra)
        put_dot(j, 6, pa2w, pa2)
        bw = weighted(planes_of(B))
        put_dot(j, 7, bw, planes_of(pa_slot))
        if j == 1:
            put_dot(j, 8, bw, ra)
            put_dot(j, 9, bw, pa2)

    def steps(j, rho):
        s = sum_finish(j)
        (ra_r, ra_pa, ra_ra, p2_r, p2_pa, p2_ra, p2_p2, b_pa, b_ra, b_p2) = [
            s[i : i + 1] for i in range(10)
        ]
        alpha = rho / b_pa
        cross = ra_r - alpha * (ra_pa + p2_r) + alpha * alpha * p2_pa
        square = ra_ra - 2.0 * alpha * p2_ra + alpha * alpha * p2_p2
        omega = cross / square
        rho_next = -omega * (b_ra - alpha * b_p2)
        beta = rho_next / rho * (alpha / omega)
        return alpha, omega, beta, rho_next

    put_dots(1)
    sum_start(1)
    apply_rest(PA2, 5)
    sum_middle(1)
    halo_finish(5, PA3)
    apply_edges(PA3, 6)
    apply_rest(PA3, 6)
    for x in range(8):
        put(vec.at[RA3], x, get(vec.at[PA3], x) - be * (get(vec.at[V3], x) - om * get(vec.at[V4], x)))
    halo_finish(6, PA4)

    alpha, omega, beta, rho = steps(1, rho)
    al, om, be = wide_of(alpha), wide_of(omega), wide_of(beta)
    for x in range(8):
        r0, r1, r2, r3 = [get(vec.at[i], x) for i in (R, RA, RA2, RA3)]
        p0, p1, p2, p3, p4 = [get(vec.at[i], x) for i in (PP, PA, PA2, PA3, PA4)]
        s0 = r0 - al * p1
        s1 = r1 - al * p2
        s2 = r2 - al * p3
        s3 = r3 - al * p4
        r0 = s0 - om * s1
        r1 = s1 - om * s2
        r2 = s2 - om * s3
        put(vec.at[NR], x, r0)
        put(vec.at[RA], x, r1)
        put(vec.at[NPA], x, r1 + be * (p1 - om * p2))
        put(vec.at[PA2], x, r2 + be * (p2 - om * p3))

    put_dots(2)
    sum_start(2)
    for x in range(8):
        r, p0, p1, r0 = [get(vec.at[i], x) for i in (R, PP, PA, NR)]
        x_out[x] = get(vec.at[X], x) + al * p0 + om * (r - al * p1)
        pp_out[x] = r0 + be * (p0 - om * p1)
        r_out[x] = r0
        pa_out[x] = get(vec.at[NPA], x)
        ra_out[x] = get(vec.at[RA], x)
        pa2_out[x] = get(vec.at[PA2], x)
    sum_middle(2)
    alpha, omega, _, _ = steps(2, rho)
    al_out[...] = wide_of(alpha)
    om_out[...] = wide_of(omega)

    pltpu.make_async_copy(xr, xr, send_x).wait()
    pltpu.make_async_copy(yr, yr, send_y).wait()
    lines = cr.at[:, 0, :, pl.ds(0, 4), :]
    pltpu.make_async_copy(lines, lines, send_c).wait()
    sent_1 = buf1.at[:, pl.ds(0, nx - 1)]
    pltpu.make_async_copy(sent_1, sent_1, send_1).wait()
    sent_2 = buf2.at[:, pl.ds(0, ny - 1)]
    pltpu.make_async_copy(sent_2, sent_2, send_2).wait()


def constants(nz):
    w = np.array(gll_weights)
    wz = np.tile(w, nz // 8)
    node = np.arange(nz) % 8
    elem = np.arange(nz) // 8
    shared = ((node == 7) & (elem < nz // 8 - 1)) | ((node == 0) & (elem > 0))
    inv_z = np.where(shared, 0.5, 1.0)
    planes = np.stack(
        [
            w[:, None] * wz[None, :],
            np.broadcast_to(inv_z, (8, nz)),
            np.broadcast_to(w[:, None], (8, nz)),
            np.broadcast_to(wz, (8, nz)),
        ]
    ).astype(np.float32)
    mats = []
    for small in (D.T, D):
        rest = np.kron(np.eye(16), small).astype(np.float32)
        parts = []
        for _ in range(3):
            part = rest.astype(jnp.bfloat16)
            parts.append(part)
            rest = rest - part.astype(np.float32)
        d1, d2, d3 = parts
        both = np.concatenate([d1, d2], axis=1)
        last = np.concatenate([d1, d3], axis=0)
        mats.append(
            np.stack(
                [
                    np.concatenate([both, both], axis=0),
                    np.concatenate([last, np.zeros_like(last)], axis=1),
                ]
            )
        )
    return np.stack(mats), planes


def solution(mesh):
    nx, ny = mesh.shape["gx"], mesh.shape["gy"]

    def per_device(source, conductivity, robin_flags, htc_class, htc_table):
        nz = source.shape[2]
        ez = robin_flags.shape[2]
        mats, planes = constants(nz)
        any_spec = pl.BlockSpec(memory_space=pl.ANY)
        vm = pltpu.VMEM
        dma = pltpu.SemaphoreType.DMA
        field = (8, 8, nz)
        nt = nz // 128
        flat = (nt, 64, 128)
        x, pp, r, pa, ra, pa2, alpha, omega = pl.pallas_call(
            functools.partial(kernel, nx, ny, nz),
            out_shape=(pltpu.VMEM(field, f32),) * 6 + (pltpu.VMEM((8, nz), f32),) * 2,
            in_specs=[any_spec] * 7,
            out_specs=(pl.BlockSpec(memory_space=pltpu.VMEM),) * 8,
            scratch_shapes=[
                vm(field, f32),
                vm((2, 8, nz), f32),
                vm(field, f32),
                vm(field, f32),
                vm(flat, f32),
                vm(flat, f32),
                vm((1, ez), jnp.int32),
                vm((1, ez), jnp.int32),
                pltpu.SMEM((1, 4), f32),
                vm((2, 2, 256, 256), jnp.bfloat16),
                vm((4, 8, nz), f32),
                vm(flat, f32),
                vm(flat, f32),
                vm((ROUNDS,) + flat, f32),
                vm((17,) + flat, f32),
                vm(flat, f32),
                vm(flat, f32),
                vm(flat, f32),
                vm((16 * nt, 128), f32),
                vm((ROUNDS, 2, nt, 8, 128), f32),
                vm((ROUNDS, 2, nt, 8, 128), f32),
                vm((ROUNDS, 2, nt, 8, 128), f32),
                vm((ROUNDS, 2, nt, 8, 128), f32),
                vm((SUMS, 128, 128), f32),
                vm((SUMS, 1, 128), f32),
                vm((SUMS, 1, 128), f32),
                vm((SUMS, nx, 1, 128), f32),
                vm((SUMS, ny, 1, 128), f32),
                dma((11,)),
                dma,
                dma,
                dma,
                dma((ROUNDS,)),
                dma((ROUNDS,)),
                dma((ROUNDS,)),
                dma,
                dma,
                dma((SUMS,)),
                dma((SUMS,)),
            ],
            compiler_params=pltpu.CompilerParams(collective_id=0, has_side_effects=True),
        )(
            source,
            conductivity,
            robin_flags.reshape(1, ez),
            htc_class.reshape(1, ez),
            htc_table.reshape(1, 4),
            mats,
            planes,
        )
        half = r - alpha * pa
        return x + alpha * pp + omega * half, half - omega * (ra - alpha * pa2)

    return jax.shard_map(
        per_device,
        mesh=mesh,
        in_specs=(
            P("gx", "gy", None),
            P("gx", "gy", None),
            P("gx", "gy", None),
            P("gx", "gy", None),
            P(),
        ),
        out_specs=(P("gx", "gy", None), P("gx", "gy", None)),
        check_vma=False,
    )
```

```python
import functools

import jax
import jax.numpy as jnp
import numpy as np
from jax import lax
from jax.experimental import pallas as pl
from jax.experimental.pallas import tpu as pltpu
from jax.sharding import PartitionSpec as P

MESH = pl.DeviceIdType.MESH
HIGHEST = lax.Precision.HIGHEST
f32 = jnp.float32

gll_points = (
    -1.0,
    -0.8717401485096066,
    -0.5917001814331423,
    -0.2092992179024789,
    0.2092992179024789,
    0.5917001814331423,
    0.8717401485096066,
    1.0,
)
gll_weights = (
    0.03571428571428571,
    0.21070422714350603,
    0.3411226924835044,
    0.4124587946587038,
    0.4124587946587038,
    0.3411226924835044,
    0.21070422714350603,
    0.03571428571428571,
)
mass_coef = 0.2
scan_speed = 2.0
ROUNDS = 7
SUMS = 3


def derivative_matrix():
    points = np.array(gll_points)
    bary = np.array(
        [1.0 / np.prod([points[j] - points[m] for m in range(8) if m != j]) for j in range(8)]
    )
    d = np.zeros((8, 8))
    for a in range(8):
        for b in range(8):
            if a != b:
                d[a, b] = bary[b] / bary[a] / (points[a] - points[b])
        d[a, a] = -np.sum(d[a])
    return d


D = derivative_matrix()


def along_planes(planes, mat):
    even = [planes[b] + planes[7 - b] for b in range(4)]
    odd = [planes[b] - planes[7 - b] for b in range(4)]
    out = [None] * 8
    for a in range(4):
        p = sum(float(0.5 * (mat[a, b] + mat[a, 7 - b])) * even[b] for b in range(4))
        q = sum(float(0.5 * (mat[a, b] - mat[a, 7 - b])) * odd[b] for b in range(4))
        out[a] = p + q
        out[7 - a] = q - p
    return out


def ends(planes, mat):
    even = [planes[b] + planes[7 - b] for b in range(4)]
    odd = [planes[b] - planes[7 - b] for b in range(4)]
    p = sum(float(0.5 * (mat[0, b] + mat[0, 7 - b])) * even[b] for b in range(4))
    q = sum(float(0.5 * (mat[0, b] - mat[0, 7 - b])) * odd[b] for b in range(4))
    return p + q, q - p


def kernel(
    nx, ny, nz,
    src_hbm, cond_hbm, flags_hbm, class_hbm, table_hbm, mats_hbm, planes_hbm,
    x_out, pp_out, r_out, pa_out, ra_out, pa2_out, al_out, om_out,
    src, rows, cond, w2, wk, wkt, flags, classes, table, mats, planes, mass, im,
    loc, vec, tmp, fx, fy, ywk, ymass, xr, yr, cr, ysend,
    parts, msg1, msg2, buf1, buf2,
    in_sem, send_x, send_y, send_c, recv_x, recv_y, recv_c,
    send_1, send_2, recv_1, recv_2,
):
    gx = lax.axis_index("gx")
    gy = lax.axis_index("gy")

    def at_x(k):
        return (gx + (k % nx)) & (nx - 1)

    def at_y(k):
        return (gy + (k % ny)) & (ny - 1)

    loads = [
        pltpu.make_async_copy(a, b, in_sem.at[i])
        for i, (a, b) in enumerate(
            [
                (src_hbm.at[:, 0, :], rows.at[0]),
                (src_hbm.at[:, 7, :], rows.at[1]),
                (src_hbm.at[0], src.at[0]),
                (src_hbm.at[7], src.at[7]),
                (planes_hbm, planes),
                (src_hbm.at[pl.ds(1, 6)], src.at[pl.ds(1, 6)]),
                (cond_hbm, cond),
                (mats_hbm, mats),
                (flags_hbm, flags),
                (class_hbm, classes),
                (table_hbm, table),
            ]
        )
    ]
    for c in loads[:6]:
        c.start()

    barrier = pltpu.get_barrier_semaphore()
    order_x = sorted(range(1, nx), key=lambda k: abs(k - nx // 2))
    order_y = sorted(range(1, ny), key=lambda k: abs(k - ny // 2))
    peers = [(at_x(dx), at_y(dy)) for dx in (-1, 1) for dy in (-1, 1)]
    peers += [(gx, at_y(k)) for k in order_y] + [(at_x(k), gy) for k in order_x]
    for peer in peers:
        pl.semaphore_signal(barrier, inc=1, device_id=peer, device_id_type=MESH)
    for c in loads[6:]:
        c.start()

    lane = lax.broadcasted_iota(jnp.int32, (8, nz), 1)
    node_z = lax.rem(lane, 8)
    row = lax.broadcasted_iota(jnp.int32, (8, nz), 0)
    join_up = (node_z == 7) & (lane < nz - 1)
    join_dn = (node_z == 0) & (lane > 0)
    zero = jnp.zeros((8, nz), f32)
    x_lo, x_hi = gx > 0, gx < nx - 1
    y_lo, y_hi = gy > 0, gy < ny - 1
    row_t = lax.broadcasted_iota(jnp.int32, (8, 128), 0)
    corner = ((row_t == 0) & x_lo) | ((row_t == 7) & x_hi)
    tile0 = jnp.zeros((8, 128), f32)
    chunks = [slice(128 * t, 128 * t + 128) for t in range(nz // 128)]

    def zfold(plane):
        up = pltpu.roll(plane, nz - 1, 1)
        dn = pltpu.roll(plane, 1, 1)
        return plane + jnp.where(join_up, up, jnp.where(join_dn, dn, zero))

    nt = len(chunks)

    def at(x):
        return slice(8 * x, 8 * x + 8)

    def get(ref, x):
        return jnp.concatenate([ref[t, at(x), :] for t in range(nt)], axis=1)

    def put(ref, x, plane):
        for t, c in enumerate(chunks):
            ref[t, at(x), :] = plane[:, c]

    def across(y):
        return pl.ds(y, 8, stride=8)

    for c in loads[:5]:
        c.wait()
    w_yz = planes[0]
    inv_z = planes[1]

    def send(s, d, ss, rs, peer):
        pltpu.make_async_remote_copy(
            src_ref=s, dst_ref=d, send_sem=ss, recv_sem=rs,
            device_id=peer, device_id_type=MESH,
        ).start()

    def y_start(k):
        for dx, dy in ((-1, -1), (-1, 1), (1, -1), (1, 1)):
            send(
                ysend.at[k, int(dy > 0), :, pl.ds(7 * (dx > 0), 1), :],
                cr.at[k, int(dy < 0), :, pl.ds(7 * (dx < 0), 1), :],
                send_c, recv_c.at[k], (at_x(dx), at_y(dy)),
            )
        for i, dy in enumerate((-1, 1)):
            send(ysend.at[k, i], yr.at[k, 1 - i], send_y, recv_y.at[k], (gx, at_y(dy)))

    def x_start(k):
        for i, dx in enumerate((-1, 1)):
            send(
                loc.at[k, :, pl.ds(56 * i, 8), :], xr.at[k, 1 - i],
                send_x, recv_x.at[k], (at_x(dx), gy),
            )

    def halo_finish(k, dst):
        for t in range(nt):
            vec[dst, t, 8:56, :] = loc[k, t, 8:56, :]
        pltpu.make_async_copy(xr.at[k], xr.at[k], recv_x.at[k]).wait()
        for t in range(nt):
            vec[dst, t, at(0), :] = loc[k, t, at(0), :] + jnp.where(x_lo, xr[k, 0, t], tile0)
            vec[dst, t, at(7), :] = loc[k, t, at(7), :] + jnp.where(x_hi, xr[k, 1, t], tile0)
        pltpu.make_async_copy(yr.at[k], yr.at[k], recv_y.at[k]).wait()
        lines = cr.at[k, 0, :, pl.ds(0, 4), :]
        pltpu.make_async_copy(lines, lines, recv_c.at[k]).wait()
        for i, has in enumerate((y_lo, y_hi)):
            for t in range(nt):
                add = yr[k, i, t] + jnp.where(corner, cr[k, i, t], tile0)
                add = jnp.where(has, add, tile0)
                vec.at[dst, t][across(7 * i), :] = vec.at[dst, t][across(7 * i), :] + add

    end = float(gll_weights[0])
    for i in (0, 1):
        face = zfold(end * w_yz * rows[i])
        for t, c in enumerate(chunks):
            ysend[0, i, t] = face[:, c]
        put(loc.at[0], 7 * i, zfold(end * w_yz * src[7 * i]))
    pl.semaphore_wait(barrier, len(peers))
    y_start(0)
    x_start(0)
    loads[5].wait()
    for x in range(1, 7):
        put(loc.at[0], x, zfold(float(gll_weights[x]) * w_yz * src[x]))

    for c in loads[6:]:
        c.wait()
    bits = flags[...]
    kinds = classes[...]
    coef = jnp.zeros(kinds.shape, f32)
    for i in range(4):
        coef = coef + jnp.where(kinds == i, table[0, i], 0.0)
    edge = [gx == 0, gx == nx - 1, gy == 0, gy == ny - 1]
    faces = []
    for i in range(6):
        bit = lax.bitwise_and(lax.shift_right_logical(bits, i), 1).astype(f32)
        face = coef * bit
        if i < 4:
            face = jnp.where(edge[i], face, 0.0)
        faces.append(face)
    faces = jnp.concatenate(faces + [jnp.zeros((2, kinds.shape[1]), f32)], axis=0)
    elem = lax.broadcasted_iota(jnp.int32, (kinds.shape[1], nz), 0)
    spread = (lax.broadcasted_iota(jnp.int32, (kinds.shape[1], nz), 1) // 8 == elem).astype(f32)
    wide = jnp.dot(faces, spread, precision=HIGHEST, preferred_element_type=f32)

    def line(i):
        return jnp.broadcast_to(wide[i : i + 1], (8, nz))

    w_y = planes[2]
    w_z = planes[3]
    side_y = jnp.where(row == 0, line(2), jnp.where(row == 7, line(3), zero)) * w_z
    side_z = jnp.where(lane == 0, line(4), jnp.where(lane == nz - 1, line(5), zero)) * w_y
    inv_y = jnp.where(((row == 0) & y_lo) | ((row == 7) & y_hi), 0.5, 1.0).astype(f32)
    inv_yz = inv_y * inv_z
    for x in range(8):
        wx = float(gll_weights[x])
        robin = wx * (side_y + side_z)
        inv = inv_yz
        if x == 0:
            robin = robin + line(0) * w_yz
            inv = jnp.where(x_lo, 0.5 * inv_yz, inv_yz)
        if x == 7:
            robin = robin + line(1) * w_yz
            inv = jnp.where(x_hi, 0.5 * inv_yz, inv_yz)
        put(mass, x, (mass_coef * wx) * w_yz + robin)
        put(im, x, inv)
        w2[x] = (scan_speed * wx) * w_yz
        put(wk, x, (wx * w_yz) * cond[x])
    for t in range(nt):
        for y in range(8):
            wkt[t, at(y), :] = wk.at[t][across(y), :]
        for i in (0, 1):
            ywk[pl.ds(8 * (i * nt + t), 8), :] = wk.at[t][across(7 * i), :]
            ymass[pl.ds(8 * (i * nt + t), 8), :] = mass.at[t][across(7 * i), :]

    bf = jnp.bfloat16

    def pieces(v):
        h1 = v.astype(bf)
        rest = v - h1.astype(f32)
        h2 = rest.astype(bf)
        h3 = (rest - h2.astype(f32)).astype(bf)
        return jnp.concatenate([h1, h2], axis=1), jnp.concatenate([h3, h1], axis=1)

    def along_z(v, i):
        first, second = pieces(v)
        one = jnp.dot(first, mats[i, 0], preferred_element_type=f32)
        two = jnp.dot(second, mats[i, 1, :, 0:128], preferred_element_type=f32)
        return one[:, 0:128] + (one[:, 128:256] + two)

    def apply_edges(s, k):
        rows = jnp.concatenate(
            [vec.at[s, t][across(7 * i), :] for i in (0, 1) for t in range(nt)], axis=0
        )
        face_z = along_z(ywk[...] * along_z(rows, 0), 1)
        face_y = [[], []]
        for t in range(nt):
            turned = [vec.at[s, t][across(y), :] for y in range(8)]
            grad = along_planes(turned, D)
            flux = [wkt[t, at(y), :] * grad[y] for y in range(8)]
            for y in range(8):
                fy[t, at(y), :] = flux[y]
            for i, end in enumerate(ends(flux, D.T)):
                face_y[i].append(end)
            v = [vec[s, t, at(x), :] for x in range(8)]
            grad = along_planes(v, D)
            flux = [wk[t, at(x), :] * grad[x] - w2[x, :, chunks[t]] * v[x] for x in range(8)]
            back = along_planes(flux, D.T)
            for x in range(8):
                fx[t, at(x), :] = back[x]
        for i in (0, 1):
            face = [
                fx.at[t][across(7 * i), :]
                + face_y[i][t]
                + face_z[8 * (i * nt + t) : 8 * (i * nt + t) + 8]
                + ymass[pl.ds(8 * (i * nt + t), 8), :] * vec.at[s, t][across(7 * i), :]
                for t in range(nt)
            ]
            face = zfold(jnp.concatenate(face, axis=1))
            for t, c in enumerate(chunks):
                ysend[k, i, t] = face[:, c]
        y_start(k)

    def apply_rest(s, k):
        grad_z = along_z(vec[s].reshape(64 * nt, 128), 0)
        back_z = along_z(wk[...].reshape(64 * nt, 128) * grad_z, 1)
        for t in range(nt):
            back = along_planes([fy[t, at(y), :] for y in range(8)], D.T)
            for y in range(8):
                tmp.at[t][across(y), :] = back[y]
        for x in range(8):
            side = jnp.concatenate(
                [back_z[64 * t + 8 * x : 64 * t + 8 * x + 8] for t in range(nt)], axis=1
            )
            local = get(mass, x) * get(vec.at[s], x) + get(fx, x)
            put(loc.at[k], x, zfold(get(tmp, x) + local + side))
        x_start(k)

    parts[...] = jnp.zeros(parts.shape, f32)
    ones = jnp.ones((8, 128), f32)

    def put_dot(j, d, left, right):
        total = sum(left[x] * right[x] for x in range(8))
        parts[j, 8 * d : 8 * d + 8, :] = sum(total[:, c] for c in chunks)

    def planes_of(s):
        return [get(vec.at[s], x) for x in range(8)]

    def weighted(v):
        return [get(im, x) * v[x] for x in range(8)]

    def sum_start(j):
        rows = lax.dot_general(
            ones, parts[j], (((1,), (1,)), ((), ())),
            precision=HIGHEST, preferred_element_type=f32,
        )
        msg1[j] = rows[0:1]
        buf1[j, pl.ds(gx, 1)] = rows[0:1].reshape(1, 1, 128)
        for k in order_x:
            pltpu.make_async_remote_copy(
                src_ref=msg1.at[j], dst_ref=buf1.at[j, gx], send_sem=send_1,
                recv_sem=recv_1.at[j], device_id=(at_x(k), gy), device_id_type=MESH,
            ).start()

    def sum_middle(j):
        pltpu.make_async_copy(
            buf1.at[j, pl.ds(0, nx - 1)], buf1.at[j, pl.ds(0, nx - 1)], recv_1.at[j]
        ).wait()
        total = jnp.sum(buf1[j], axis=0)
        msg2[j] = total
        buf2[j, pl.ds(gy, 1)] = total.reshape(1, 1, 128)
        for k in order_y:
            pltpu.make_async_remote_copy(
                src_ref=msg2.at[j], dst_ref=buf2.at[j, gy], send_sem=send_2,
                recv_sem=recv_2.at[j], device_id=(gx, at_y(k)), device_id_type=MESH,
            ).start()

    pick = (
        lax.broadcasted_iota(jnp.int32, (16, 128), 1) // 8
        == lax.broadcasted_iota(jnp.int32, (16, 128), 0)
    )

    def sum_finish(j):
        pltpu.make_async_copy(
            buf2.at[j, pl.ds(0, ny - 1)], buf2.at[j, pl.ds(0, ny - 1)], recv_2.at[j]
        ).wait()
        total = jnp.broadcast_to(jnp.sum(buf2[j], axis=0), (16, 128))
        spread_rows = jnp.where(pick, total, 0.0)
        return jnp.dot(
            spread_rows, jnp.ones((128, 128), f32), precision=HIGHEST,
            preferred_element_type=f32,
        )

    def wide_of(scalar):
        return jnp.broadcast_to(jnp.concatenate([scalar] * len(chunks), axis=1), (8, nz))

    B, V1, V2, V3, V4, R, RA, RA2, RA3, PP, PA, PA2, PA3, PA4, X, NR, NPA = range(17)

    halo_finish(0, B)
    apply_edges(B, 1)
    apply_rest(B, 1)
    b = planes_of(B)
    bw = weighted(b)
    put_dot(0, 0, bw, b)
    halo_finish(1, V1)
    apply_edges(V1, 2)
    apply_rest(V1, 2)
    v1 = planes_of(V1)
    put_dot(0, 1, weighted(planes_of(B)), v1)
    put_dot(0, 2, weighted(v1), v1)
    halo_finish(2, V2)
    v2 = planes_of(V2)
    v2w = weighted(v2)
    put_dot(0, 3, v2w, planes_of(B))
    put_dot(0, 4, v2w, planes_of(V1))
    put_dot(0, 5, v2w, v2)
    sum_start(0)
    apply_edges(V2, 3)
    apply_rest(V2, 3)
    sum_middle(0)
    halo_finish(3, V3)
    apply_edges(V3, 4)
    apply_rest(V3, 4)
    halo_finish(4, V4)

    s = sum_finish(0)
    bb, bv1, v1v1, bv2, v1v2, v2v2 = [s[i : i + 1] for i in range(6)]
    rho = bb
    alpha = rho / bv1
    cross = bv1 - alpha * (v1v1 + bv2) + alpha * alpha * v1v2
    square = v1v1 - 2.0 * alpha * v1v2 + alpha * alpha * v2v2
    omega = cross / square
    rho_next = -omega * (bv1 - alpha * bv2)
    beta = rho_next / rho * (alpha / omega)
    rho = rho_next
    al, om, be = wide_of(alpha), wide_of(omega), wide_of(beta)
    for x in range(8):
        v2, v3, v4 = [get(vec.at[i], x) for i in (V2, V3, V4)]
        s2 = v2 - al * v3
        r2 = s2 - om * (v3 - al * v4)
        put(vec.at[RA2], x, r2)
        put(vec.at[PA2], x, r2 + be * (v2 - om * v3))
    apply_edges(PA2, 5)
    for x in range(8):
        b, v1, v2, v3 = [get(vec.at[i], x) for i in (B, V1, V2, V3)]
        s0 = b - al * v1
        s1 = v1 - al * v2
        put(vec.at[X], x, al * b + om * s0)
        r0 = s0 - om * s1
        r1 = s1 - om * (v2 - al * v3)
        put(vec.at[R], x, r0)
        put(vec.at[RA], x, r1)
        put(vec.at[PP], x, r0 + be * (b - om * v1))
        put(vec.at[PA], x, r1 + be * (v1 - om * v2))

    def put_dots(j):
        r_slot, pa_slot = (R, PA) if j == 1 else (NR, NPA)
        ra = planes_of(RA)
        raw = weighted(ra)
        put_dot(j, 0, raw, planes_of(r_slot))
        put_dot(j, 1, raw, planes_of(pa_slot))
        put_dot(j, 2, raw, ra)
        pa2 = planes_of(PA2)
        pa2w = weighted(pa2)
        put_dot(j, 3, pa2w, planes_of(r_slot))
        put_dot(j, 4, pa2w, planes_of(pa_slot))
        put_dot(j, 5, pa2w, ra)
        put_dot(j, 6, pa2w, pa2)
        bw = weighted(planes_of(B))
        put_dot(j, 7, bw, planes_of(pa_slot))
        if j == 1:
            put_dot(j, 8, bw, ra)
            put_dot(j, 9, bw, pa2)

    def steps(j, rho):
        s = sum_finish(j)
        (ra_r, ra_pa, ra_ra, p2_r, p2_pa, p2_ra, p2_p2, b_pa, b_ra, b_p2) = [
            s[i : i + 1] for i in range(10)
        ]
        alpha = rho / b_pa
        cross = ra_r - alpha * (ra_pa + p2_r) + alpha * alpha * p2_pa
        square = ra_ra - 2.0 * alpha * p2_ra + alpha * alpha * p2_p2
        omega = cross / square
        rho_next = -omega * (b_ra - alpha * b_p2)
        beta = rho_next / rho * (alpha / omega)
        return alpha, omega, beta, rho_next

    put_dots(1)
    sum_start(1)
    apply_rest(PA2, 5)
    sum_middle(1)
    halo_finish(5, PA3)
    apply_edges(PA3, 6)
    apply_rest(PA3, 6)
    for x in range(8):
        put(vec.at[RA3], x, get(vec.at[PA3], x) - be * (get(vec.at[V3], x) - om * get(vec.at[V4], x)))
    halo_finish(6, PA4)

    alpha, omega, beta, rho = steps(1, rho)
    al, om, be = wide_of(alpha), wide_of(omega), wide_of(beta)
    for x in range(8):
        r0, r1, r2, r3 = [get(vec.at[i], x) for i in (R, RA, RA2, RA3)]
        p0, p1, p2, p3, p4 = [get(vec.at[i], x) for i in (PP, PA, PA2, PA3, PA4)]
        s0 = r0 - al * p1
        s1 = r1 - al * p2
        s2 = r2 - al * p3
        s3 = r3 - al * p4
        r0 = s0 - om * s1
        r1 = s1 - om * s2
        r2 = s2 - om * s3
        put(vec.at[NR], x, r0)
        put(vec.at[RA], x, r1)
        put(vec.at[NPA], x, r1 + be * (p1 - om * p2))
        put(vec.at[PA2], x, r2 + be * (p2 - om * p3))

    put_dots(2)
    sum_start(2)
    for x in range(8):
        r, p0, p1, r0 = [get(vec.at[i], x) for i in (R, PP, PA, NR)]
        x_out[x] = get(vec.at[X], x) + al * p0 + om * (r - al * p1)
        pp_out[x] = r0 + be * (p0 - om * p1)
        r_out[x] = r0
        pa_out[x] = get(vec.at[NPA], x)
        ra_out[x] = get(vec.at[RA], x)
        pa2_out[x] = get(vec.at[PA2], x)
    sum_middle(2)
    alpha, omega, _, _ = steps(2, rho)
    al_out[...] = wide_of(alpha)
    om_out[...] = wide_of(omega)

    pltpu.make_async_copy(xr, xr, send_x).wait()
    pltpu.make_async_copy(yr, yr, send_y).wait()
    lines = cr.at[:, 0, :, pl.ds(0, 4), :]
    pltpu.make_async_copy(lines, lines, send_c).wait()
    sent_1 = buf1.at[:, pl.ds(0, nx - 1)]
    pltpu.make_async_copy(sent_1, sent_1, send_1).wait()
    sent_2 = buf2.at[:, pl.ds(0, ny - 1)]
    pltpu.make_async_copy(sent_2, sent_2, send_2).wait()


def constants(nz):
    w = np.array(gll_weights)
    wz = np.tile(w, nz // 8)
    node = np.arange(nz) % 8
    elem = np.arange(nz) // 8
    shared = ((node == 7) & (elem < nz // 8 - 1)) | ((node == 0) & (elem > 0))
    inv_z = np.where(shared, 0.5, 1.0)
    planes = np.stack(
        [
            w[:, None] * wz[None, :],
            np.broadcast_to(inv_z, (8, nz)),
            np.broadcast_to(w[:, None], (8, nz)),
            np.broadcast_to(wz, (8, nz)),
        ]
    ).astype(np.float32)
    mats = []
    for small in (D.T, D):
        rest = np.kron(np.eye(16), small).astype(np.float32)
        parts = []
        for _ in range(3):
            part = rest.astype(jnp.bfloat16)
            parts.append(part)
            rest = rest - part.astype(np.float32)
        d1, d2, d3 = parts
        both = np.concatenate([d1, d2], axis=1)
        last = np.concatenate([d1, d3], axis=0)
        mats.append(
            np.stack(
                [
                    np.concatenate([both, both], axis=0),
                    np.concatenate([last, np.zeros_like(last)], axis=1),
                ]
            )
        )
    return np.stack(mats), planes


def solution(mesh):
    nx, ny = mesh.shape["gx"], mesh.shape["gy"]

    def per_device(source, conductivity, robin_flags, htc_class, htc_table):
        nz = source.shape[2]
        ez = robin_flags.shape[2]
        mats, planes = constants(nz)
        any_spec = pl.BlockSpec(memory_space=pl.ANY)
        vm = pltpu.VMEM
        dma = pltpu.SemaphoreType.DMA
        field = (8, 8, nz)
        nt = nz // 128
        flat = (nt, 64, 128)
        x, pp, r, pa, ra, pa2, alpha, omega = pl.pallas_call(
            functools.partial(kernel, nx, ny, nz),
            out_shape=(pltpu.VMEM(field, f32),) * 6 + (pltpu.VMEM((8, nz), f32),) * 2,
            in_specs=[any_spec] * 7,
            out_specs=(pl.BlockSpec(memory_space=pltpu.VMEM),) * 8,
            scratch_shapes=[
                vm(field, f32),
                vm((2, 8, nz), f32),
                vm(field, f32),
                vm(field, f32),
                vm(flat, f32),
                vm(flat, f32),
                vm((1, ez), jnp.int32),
                vm((1, ez), jnp.int32),
                pltpu.SMEM((1, 4), f32),
                vm((2, 2, 256, 256), jnp.bfloat16),
                vm((4, 8, nz), f32),
                vm(flat, f32),
                vm(flat, f32),
                vm((ROUNDS,) + flat, f32),
                vm((17,) + flat, f32),
                vm(flat, f32),
                vm(flat, f32),
                vm(flat, f32),
                vm((16 * nt, 128), f32),
                vm((16 * nt, 128), f32),
                vm((ROUNDS, 2, nt, 8, 128), f32),
                vm((ROUNDS, 2, nt, 8, 128), f32),
                vm((ROUNDS, 2, nt, 8, 128), f32),
                vm((ROUNDS, 2, nt, 8, 128), f32),
                vm((SUMS, 128, 128), f32),
                vm((SUMS, 1, 128), f32),
                vm((SUMS, 1, 128), f32),
                vm((SUMS, nx, 1, 128), f32),
                vm((SUMS, ny, 1, 128), f32),
                dma((11,)),
                dma,
                dma,
                dma,
                dma((ROUNDS,)),
                dma((ROUNDS,)),
                dma((ROUNDS,)),
                dma,
                dma,
                dma((SUMS,)),
                dma((SUMS,)),
            ],
            compiler_params=pltpu.CompilerParams(collective_id=0, has_side_effects=True),
        )(
            source,
            conductivity,
            robin_flags.reshape(1, ez),
            htc_class.reshape(1, ez),
            htc_table.reshape(1, 4),
            mats,
            planes,
        )
        half = r - alpha * pa
        return x + alpha * pp + omega * half, half - omega * (ra - alpha * pa2)

    return jax.shard_map(
        per_device,
        mesh=mesh,
        in_specs=(
            P("gx", "gy", None),
            P("gx", "gy", None),
            P("gx", "gy", None),
            P("gx", "gy", None),
            P(),
        ),
        out_specs=(P("gx", "gy", None), P("gx", "gy", None)),
        check_vma=False,
    )
```
